512 devices in a mesh: pool: 2 (over x_hi), slab: 128 (over z, x_lo, y), ch: 2 (over core).
Axes of the slice: x: 4 (x_hi: 2, x_lo: 2; x = x_hi * 2 + x_lo), y: 4, z: 16, core: 2. Of those that a mesh axis runs over, the one named last changes fastest.
Arguments:
- fields: bfloat16 [2, 20, 256, 224, 128], P('pool', 'ch', 'slab'), may hold values from -6 to 6
- mode_weights: bfloat16 [2, 20, 20, 64, 4096], P('pool', 'ch', None, None, 'slab'), may hold values from -1.25 to 1.25
- lin_weights: bfloat16 [2, 20, 20], P('pool', None, 'ch'), may hold values from -1.25 to 1.25
- bias: bfloat16 [2, 20], P('pool', 'ch'), may hold values from -1 to 1
- source: int32 [128, 8], P('slab'), may hold values from -1 to 127, as said below
Outputs:
- fields_out: bfloat16 [2, 20, 256, 224, 128], P('pool', 'ch', 'slab')
The draws below stay inside these ranges and needn't reach their ends.
Inputs may be any that keep to these rules, and one draw needn't show every extreme that they name: source[s, b] is -1 (block not listed) or one of s - 1, s, s + 1; each row holds at most 2 entries equal to s - 1 and at most 2 equal to s + 1, and some row holds exactly 2 of each.
All inputs are finite; a program needn't handle non-finite values.
Results may differ from the reference program's by a relative error of at most 0.0055.
Values may be sent and summed in bfloat16 or wider, within the bound.
A program may use at most 64 MiB of HBM per device.

```python
import jax
import jax.numpy as jnp
from jax import lax

C = 20
NX = 256
NY = 224
NZ = 128
M = 64
NB = 8
HOP = 2
ITERS = 1
SLABS = 128
MM = 4096


def draw_source(key, part):
    base = jax.random.fold_in(key, 17)
    key_perm, key_low, key_high, key_full, key_keep = jax.random.split(base, 5)
    slab_ids = jnp.arange(SLABS, dtype=jnp.int32)[:, None]
    row_keys = jax.random.split(key_perm, SLABS)
    perms = jax.vmap(lambda single: jax.random.permutation(single, NB))(row_keys)
    ranks = jax.vmap(lambda order: jnp.zeros(NB, jnp.int32).at[order].set(jnp.arange(NB, dtype=jnp.int32)))(perms)
    lower = jax.random.randint(key_low, (SLABS, 1), 0, HOP + 1)
    upper = jax.random.randint(key_high, (SLABS, 1), 0, HOP + 1)
    full_row = jax.random.randint(key_full, (), 1, SLABS - 1)
    lower = jnp.where(slab_ids == full_row, HOP, lower)
    upper = jnp.where(slab_ids == full_row, HOP, upper)
    keeping = jax.random.randint(key_keep, (SLABS, NB), 0, 2)
    value = jnp.where(ranks < lower, slab_ids - 1, jnp.where(ranks < lower + upper, slab_ids + 1, jnp.where(keeping == 1, slab_ids, -1)))
    value = jnp.where(value >= SLABS, -1, value)
    return value.astype(jnp.int32)


def level_of(own_key, dims, shards, low, top_value):
    gain, own = 1.0, jax.random.fold_in(own_key, 6)
    for position, parts in shards:
        steps = jnp.exp(jax.random.uniform(jax.random.fold_in(own, position), (parts,), jnp.float32, low / len(shards), top_value / len(shards)))
        gain = gain * jnp.repeat(steps, dims[position] // parts).reshape([-1 if axis == position else 1 for axis in range(len(dims))])
    return gain


def centred(rng, dims, spread, limit, pieces=(), kind=jnp.bfloat16):
    level = level_of(rng, dims, pieces, -0.22, 0.18) if pieces else 1.0
    values = jax.random.normal(rng, dims, jnp.float32) * spread * level
    return jnp.minimum(jnp.maximum(values, -limit), limit).astype(kind)


def setup_inputs(seed: int = 0) -> dict:
    key_of = jax.random.split(jax.random.key(seed), 6)
    return {
        "fields": centred(key_of[0], (2, C, NX, NY, NZ), 1.0, 6.0, ((0, 2), (1, 2), (2, 128))),
        "mode_weights": centred(key_of[1], (2, C, C, M, MM), C ** -0.5, 1.25, ((0, 2), (1, 2), (4, 128))),
        "lin_weights": centred(key_of[2], (2, C, C), C ** -0.5, 1.25, ((0, 2), (2, 2))),
        "bias": jnp.clip(jax.random.uniform(key_of[3], (2, C), jnp.float32, -1.0, 1.0) * level_of(key_of[3], (2, C), ((0, 2), (1, 2)), -0.4, 0.0), -1.0, 1.0).astype(jnp.bfloat16),
        "source": draw_source(jax.random.fold_in(key_of[5], 71), 0),
    }


def tables(length, modes):
    cells = jnp.arange(length, dtype=jnp.float32)
    order = jnp.arange(modes, dtype=jnp.int32)
    half = modes // 2
    freq = jnp.where(order < half, order, order - half + 1).astype(jnp.float32)
    angle = 2.0 * jnp.pi * freq[:, None] * cells[None, :] / length
    forward = jnp.where((order < half)[:, None], jnp.cos(angle), jnp.sin(angle))
    return forward.astype(jnp.bfloat16), (forward.T * (2.0 / length)).astype(jnp.bfloat16)


def interp_table(length):
    fine_idx = jnp.arange(length, dtype=jnp.int32)[:, None]
    coarse_idx = jnp.arange(length, dtype=jnp.int32)[None, :]
    centre = length // 4 + fine_idx // 2
    second = centre - 1 + 2 * (fine_idx % 2)
    return 0.75 * (coarse_idx == centre).astype(jnp.float32) + 0.25 * (coarse_idx == second).astype(jnp.float32)


def as_float(array):
    return array.astype(jnp.float32)


def neighbour(array, offset, axis):
    length = array.shape[axis]
    zeros = jnp.zeros_like(lax.slice_in_dim(array, 0, 1, axis=axis))
    if offset == 1:
        return jnp.concatenate([lax.slice_in_dim(array, 1, length, axis=axis), zeros], axis=axis)
    return jnp.concatenate([zeros, lax.slice_in_dim(array, 0, length - 1, axis=axis)], axis=axis)


def spectral(field, weights, all_tables):
    fwd_x, inv_x, fwd_y, inv_y, fwd_z, inv_z = all_tables
    along_y = jnp.einsum('cxyz,my->cxmz', as_float(field), as_float(fwd_y)).astype(jnp.bfloat16)
    along_z = jnp.einsum('cxmz,kz->cxmk', as_float(along_y), as_float(fwd_z)).astype(jnp.bfloat16)
    along_z = along_z.reshape(C, NX, M * M)
    coeffs = jnp.einsum('cxq,nx->cnq', as_float(along_z), as_float(fwd_x)).astype(jnp.bfloat16)
    mixed = jnp.einsum('inq,ionq->onq', as_float(coeffs), as_float(weights)).astype(jnp.bfloat16)
    back_x = jnp.einsum('onq,xn->oxq', as_float(mixed), as_float(inv_x)).astype(jnp.bfloat16)
    back_x = back_x.reshape(C, NX, M, M)
    back_z = jnp.einsum('cxmk,zk->cxmz', as_float(back_x), as_float(inv_z)).astype(jnp.bfloat16)
    return jnp.einsum('cxmz,ym->cxyz', as_float(back_z), as_float(inv_y))


def reference(fields, mode_weights, lin_weights, bias, source):
    fwd_x, inv_x = tables(NX, M)
    fwd_y, inv_y = tables(NY, M)
    fwd_z, inv_z = tables(NZ, M)
    all_tables = (fwd_x, inv_x, fwd_y, inv_y, fwd_z, inv_z)
    pmat = interp_table(NZ)
    to_fine_table = pmat.T.astype(jnp.bfloat16)
    to_coarse_table = (0.5 * pmat).astype(jnp.bfloat16)
    planes = NX // SLABS
    block_rows = NY // NB
    slab_ids = jnp.arange(SLABS, dtype=jnp.int32)[:, None]
    shape_six = (C, SLABS, planes, NB, block_rows, NZ)

    def expand(mask):
        return as_float(mask)[None, :, None, :, None, None]

    current = [fields[0], fields[1]]
    for iteration in range(ITERS):
        totals = []
        specs = []
        for pool in range(2):
            spec = spectral(current[pool], mode_weights[pool], all_tables)
            linear = jnp.einsum('io,ixyz->oxyz', as_float(lin_weights[pool]), as_float(current[pool]))
            totals.append(spec + linear + as_float(bias[pool])[:, None, None, None])
            specs.append(spec)
        to_fine = jnp.dot(current[0], to_fine_table, preferred_element_type=jnp.float32).astype(jnp.bfloat16)
        to_coarse = jnp.dot(specs[1].astype(jnp.bfloat16), to_coarse_table, preferred_element_type=jnp.float32).astype(jnp.bfloat16)
        coarse_blocks = as_float(to_fine).reshape(shape_six)
        fine_blocks = as_float(to_coarse).reshape(shape_six)
        here = expand(source == slab_ids)
        fine_add = coarse_blocks * here
        coarse_add = fine_blocks * here
        for offset in (-1, 1):
            fine_add = fine_add + neighbour(coarse_blocks, offset, 1) * expand(source == slab_ids + offset)
            coarse_add = coarse_add + neighbour(fine_blocks, offset, 1) * expand(neighbour(source, offset, 0) == slab_ids)
        new_coarse = jax.nn.gelu(totals[0] + coarse_add.reshape(C, NX, NY, NZ), approximate=False).astype(jnp.bfloat16)
        new_fine = jax.nn.gelu(totals[1] + fine_add.reshape(C, NX, NY, NZ), approximate=False).astype(jnp.bfloat16)
        current = [new_coarse, new_fine]
    return jnp.stack(current)
```

```python
import functools

import jax
import jax.numpy as jnp
import numpy as np
from jax import lax
from jax.experimental import pallas as pl
from jax.experimental.pallas import tpu as pltpu
from jax.sharding import PartitionSpec as P

MESH = pl.DeviceIdType.MESH
BF16 = jnp.bfloat16
F32 = jnp.float32

CH, PLANES, NY, NZ, M = 10, 2, 224, 128, 64
NX = 256
RZ, RW = 16, 8
PC = CH * PLANES
LANES = PC * 32
BLOCKS, ROWS = 8, 28
PACKED = CH * 128 + 128
NAMES = ("fy", "gy", "fx", "gx", "bdf", "bdi", "bdc", "perm_a", "perm_b", "pack", "unpack")


def dft(length):
    cells = np.arange(length, dtype=np.float32)
    order = np.arange(M, dtype=np.int32)
    half = M // 2
    freq = np.where(order < half, order, order - half + 1).astype(np.float32)
    angle = np.float32(2.0 * np.pi) * freq[:, None] * cells[None, :] / np.float32(length)
    forward = np.where((order < half)[:, None], np.cos(angle), np.sin(angle)).astype(np.float32)
    return forward, (forward.T * np.float32(2.0 / length)).astype(np.float32)


def rounded(array):
    return np.asarray(array, np.float32).astype(BF16)


def interp():
    fine = np.arange(NZ)[:, None]
    coarse = np.arange(NZ)[None, :]
    centre = NZ // 4 + fine // 2
    second = centre - 1 + 2 * (fine % 2)
    return (0.75 * (coarse == centre) + 0.25 * (coarse == second)).astype(np.float32)


def make_tables():
    fwd_x, inv_x = (rounded(table).astype(np.float32) for table in dft(NX))
    fwd_y, inv_y = (rounded(table).astype(np.float32) for table in dft(NY))
    fwd_z, inv_z = (rounded(table).astype(np.float32) for table in dft(NZ))
    mat = interp()
    inv_c = (0.5 * mat).T @ inv_z
    bdf = np.zeros((4, NZ, 2, 4, 32), np.float32)
    bdi = np.zeros((2, 4, 32, 4, NZ), np.float32)
    bdc = np.zeros((2, 4, 32, 4, NZ), np.float32)
    for group in range(4):
        for half in range(2):
            part = slice(half * 32, half * 32 + 32)
            bdf[group, :, half, group, :] = fwd_z[part].T
            bdi[half, group, :, group, :] = inv_z[:, part].T
            bdc[half, group, :, group, :] = inv_c[:, part].T
    perm_a = np.zeros((128, 128), np.float32)
    perm_b = np.zeros((128, 128), np.float32)
    for z in range(RZ):
        for w in range(RW):
            perm_a[z * 8 + w, (w % 2) * 64 + z * 4 + w // 2] = 1.0
            perm_b[w * 16 + z, z * 8 + w] = 1.0
    fx = np.zeros((2, 128, M), np.float32)
    gx = np.zeros((2, 128, M), np.float32)
    for z in range(RZ):
        for w in range(RW):
            for plane in range(2):
                cell = 2 * (z * 8 + w) + plane
                fx[plane, w * 16 + z] = fwd_x[:, cell]
                gx[plane, w * 16 + z] = inv_x[cell]
    pack = np.zeros((2, NZ, 128), np.float32)
    unpack = np.zeros((128, 2, NZ), np.float32)
    for plane in range(2):
        for cell in range(64):
            pack[plane, 32 + cell, plane * 64 + cell] = 1.0
            unpack[plane * 64 + cell, plane, :] = mat[:, 32 + cell]
    values = {
        "fy": fwd_y,
        "gy": inv_y,
        "fx": fx,
        "gx": gx,
        "bdf": bdf.reshape(512, 256),
        "bdi": bdi.reshape(256, 512),
        "bdc": bdc.reshape(256, 512),
        "perm_a": perm_a,
        "perm_b": perm_b,
        "pack": pack.reshape(256, 128),
        "unpack": unpack.reshape(128, 256),
    }
    return [rounded(values[name]) for name in NAMES]


def dot(left, right):
    return lax.dot_general(left, right, (((1,), (0,)), ((), ())), preferred_element_type=F32)


def dot_nt(left, right):
    return lax.dot_general(left, right, (((1,), (1,)), ((), ())), preferred_element_type=F32)


def dot_tn(left, right):
    return lax.dot_general(left, right, (((0,), (0,)), ((), ())), preferred_element_type=F32)


def iota(shape, axis):
    return lax.broadcasted_iota(jnp.int32, shape, axis)


def hot(mask):
    return jnp.where(mask, 1.0, 0.0)


def kernel(
    field, weights, lin, bias, source,
    fy, gy, fx, gx, bdf, bdi, bdc, perm_a, perm_b, pack, unpack,
    out,
    fld, peer, wts, along, rows_a, send_z, recv_z, send_w, recv_w, mix_send, mix_recv, mixed,
    send_v, recv_v, send_u, recv_u, codes, codes_in, base, lin_left, packed, near_send, near_recv,
    coupled, coupled_in, modes_in, left, right, result,
    load_sem, wts_sem, z_send, z_recv, w_send, w_recv, v_send, v_recv, u_send, u_recv,
    peer_sem, code_sem, mix_sem, near_sem, couple_sem, modes_sem, out_sem,
):
    pool = lax.axis_index("pool")
    slab = lax.axis_index("slab")
    ch = lax.axis_index("ch")
    zed, wid = slab // RW, lax.rem(slab, RW)
    count = RZ * RW
    above, below = lax.rem(slab + 1, count), lax.rem(slab + count - 1, count)
    is_coarse = pool == 0

    def at_z(target):
        return (pool, target * RW + wid, ch)

    def at_w(target):
        return (pool, zed * RW + target, ch)

    twin = (pool, slab, 1 - ch)
    other_pool = (1 - pool, slab, ch)
    up, down = (pool, above, ch), (pool, below, ch)

    def remote(src, dst, send, recv, device):
        return pltpu.make_async_remote_copy(
            src_ref=src, dst_ref=dst, send_sem=send, recv_sem=recv, device_id=device, device_id_type=MESH
        )

    barrier = pltpu.get_barrier_semaphore()

    def greet(device):
        pl.semaphore_signal(barrier, inc=1, device_id=device, device_id_type=MESH)

    load = pltpu.make_async_copy(field.at[0], fld, load_sem)
    load.start()
    load_w = pltpu.make_async_copy(weights, wts, wts_sem)
    load_w.start()

    @pl.loop(1, RZ)
    def _(step):
        greet(at_z(lax.rem(zed + step, RZ)))

    @pl.loop(1, RW)
    def _(step):
        greet(at_w(lax.rem(wid + step, RW)))

    for device in (twin, other_pool, up, down):
        greet(device)

    listed = source[...]
    lower = hot((listed == slab - 1) & (listed >= 0))
    upper = hot(listed == slab + 1)
    same = hot(listed == slab)
    before = hot(iota((BLOCKS, BLOCKS), 0) < iota((BLOCKS, BLOCKS), 1))
    lower_rank = dot(lower.astype(BF16), before.astype(BF16))
    upper_rank = dot(upper.astype(BF16), before.astype(BF16))
    codes[...] = jnp.full(codes.shape, -1.0, F32)
    codes[0:1, 0:BLOCKS] = jnp.where(lower > 0.5, lower_rank, -1.0)
    codes[1:2, 0:BLOCKS] = jnp.where(upper > 0.5, upper_rank, -1.0)
    codes[2:3, 0:BLOCKS] = same - 1.0

    spread = dot(
        lin[...], hot((iota((2 * CH, 256), 1) // 8) == iota((2 * CH, 256), 0)).astype(BF16)
    )
    shift = dot_tn(
        jnp.broadcast_to(bias[...], (8, CH)),
        hot((iota((8, 256), 0) == 0) & (iota((8, 256), 1) == 160)).astype(BF16),
    )
    per_row = dot(
        hot((iota((80, CH), 0) // 8) == iota((80, CH), 1)).astype(BF16), (spread + shift).astype(BF16)
    )
    keep = (lax.rem(iota((80, 256), 0), 8) == lax.rem(iota((80, 256), 1), 8)) | (
        iota((80, 256), 1) == 160
    )
    lin_left[...] = jnp.where(keep, per_row, 0.0).astype(BF16)

    load.wait()
    for pc in range(PC):
        plane, chan = pc // CH, pc % CH
        part = dot(fy[...], fld[chan, plane])
        group, lane = pc // 4, pc % 4
        along[group * 64 : group * 64 + 64, lane * 128 : lane * 128 + 128] = part.astype(BF16)
    along_z = dot(along[...], bdf[...]).astype(BF16)
    for group in range(5):
        for half in range(2):
            rows_a[half * 64 : half * 64 + 64, group * 128 : group * 128 + 128] = along_z[
                group * 64 : group * 64 + 64, half * 128 : half * 128 + 128
            ]
    send_z[...] = dot(perm_a[...], rows_a[...]).astype(BF16)

    pl.semaphore_wait(barrier, RZ - 1 + RW - 1 + 4)

    def exchange(size, mine, rows, device, src, dst, send, recv):
        def piece(ref, index):
            return ref.at[pl.ds(pl.multiple_of(index * rows, rows), rows), :]

        def copy(step):
            middle = (step + 1) // 2
            apart = size // 2 + middle * (1 - 2 * lax.rem(step, 2))
            target = lax.rem(mine + apart, size)
            return remote(piece(src, target), piece(dst, mine), send.at[target], recv.at[mine], device(target))

        def arrived(step):
            origin = lax.rem(mine + step + 1, size)
            return remote(piece(src, origin), piece(dst, origin), send.at[origin], recv.at[origin], device(origin))

        def start():
            @pl.loop(0, size - 1)
            def _(step):
                copy(step).start()

            here = pl.ds(pl.multiple_of(mine * rows, rows), rows)
            dst[here, :] = src[here, :]

        def wait_recv():
            @pl.loop(0, size - 1)
            def _(step):
                arrived(step).wait_recv()

        def wait_send():
            @pl.loop(0, size - 1)
            def _(step):
                arrived(step).wait_send()

        return start, wait_recv, wait_send

    z_start, z_wait, z_sent = exchange(RZ, zed, 8, at_z, send_z, recv_z, z_send, z_recv)
    w_start, w_wait, w_sent = exchange(RW, wid, 16, at_w, send_w, recv_w, w_send, w_recv)
    v_start, v_wait, v_sent = exchange(RW, wid, 16, at_w, send_v, recv_v, v_send, v_recv)
    u_start, u_wait, u_sent = exchange(RZ, zed, 8, at_z, send_u, recv_u, u_send, u_recv)

    z_start()
    code_up = remote(codes, codes_in.at[0], code_sem.at[0], code_sem.at[1], up)
    code_down = remote(codes, codes_in.at[1], code_sem.at[2], code_sem.at[3], down)
    code_up.start()
    code_down.start()
    to_peer = remote(fld, peer, peer_sem.at[0], peer_sem.at[1], twin)
    to_peer.start()

    near_up = remote(near_send.at[0:64], near_recv.at[0:64], near_sem.at[0], near_sem.at[1], up)
    near_down = remote(near_send.at[64:128], near_recv.at[64:128], near_sem.at[2], near_sem.at[3], down)
    couple = remote(coupled, coupled_in, couple_sem.at[0], couple_sem.at[1], other_pool)

    @pl.when(is_coarse)
    def _():
        edges = jnp.zeros((NY, 128), F32)
        for chan in range(CH):
            pair = jnp.concatenate([fld[chan, 0], fld[chan, 1]], axis=1)
            packed[:, chan * 128 : chan * 128 + 128] = dot(pair, pack[...]).astype(BF16)
            row, col = iota((256, 128), 0), iota((256, 128), 1) - 4 * chan
            pick = (
                ((row == 31) & (col == 0))
                | ((row == 96) & (col == 1))
                | ((row == 128 + 31) & (col == 2))
                | ((row == 128 + 96) & (col == 3))
            )
            edges = edges + dot(pair, hot(pick).astype(BF16))
        packed[:, CH * 128 :] = edges.astype(BF16)

    code_up.wait_recv()
    code_down.wait_recv()
    from_below, from_above = codes_in[0], codes_in[1]

    def block_columns(code):
        table = hot(iota((8, NY), 1) // ROWS == iota((8, NY), 0)).astype(BF16)
        return dot(code[:, 0:BLOCKS].astype(BF16), table)

    def block_rows(code):
        table = hot(iota((NY, 8), 0) // ROWS == iota((NY, 8), 1)).astype(BF16)
        return dot_nt(table, code[:, 0:BLOCKS].astype(BF16))

    own_rows = block_rows(codes[...])

    @pl.when(is_coarse)
    def _():
        for part, row in ((0, block_columns(from_above)[0:1]), (1, block_columns(from_below)[1:2])):
            slot, cell = iota((64, NY), 0), iota((64, NY), 1)
            pick = ((slot // ROWS).astype(F32) == row) & (lax.rem(slot, ROWS) == lax.rem(cell, ROWS))
            chosen = dot(hot(pick).astype(BF16), packed[...])
            near_send[part * 64 : part * 64 + 64, :] = chosen.astype(BF16)
        near_up.start()
        near_down.start()

    below_rows, above_rows = block_rows(from_below), block_rows(from_above)
    gy_all = gy[...].astype(F32)
    coarse_scale = jnp.where(is_coarse, 1.0, 0.0)
    left[:, 0:64] = gy[...]
    for part, mask in (
        (1, own_rows[:, 2:3]),
        (2, below_rows[:, 1:2]),
        (3, above_rows[:, 0:1]),
    ):
        left[:, part * 64 : part * 64 + 64] = (gy_all * (hot(mask > -0.5) * coarse_scale)).astype(BF16)
    right[...] = jnp.zeros(right.shape, BF16)
    mixed[...] = jnp.zeros(mixed.shape, BF16)

    z_wait()
    send_w[...] = dot(perm_b[...], recv_z[...]).astype(BF16)
    w_start()

    @pl.when(is_coarse)
    def _():
        near_up.wait_recv()
        near_down.wait_recv()
        slot, cell = iota((NY, 128), 1), iota((NY, 128), 0)
        code = jnp.where(slot < 64, own_rows[:, 0:1], own_rows[:, 1:2])
        inner = lax.rem(slot, 64)
        pick = ((inner // ROWS).astype(F32) == code) & (lax.rem(inner, ROWS) == lax.rem(cell, ROWS))
        moved = dot(hot(pick).astype(BF16), near_recv[...])
        kept = hot(own_rows[:, 2:3] > -0.5)
        coupled[...] = (moved + packed[...].astype(F32) * kept).astype(BF16)
        couple.start()

    to_peer.wait_recv()
    ones_row = hot(iota((16, 256), 0) == 0).astype(BF16)

    def channel_map(first, second):
        @pl.loop(0, NY // 8)
        def _(block):
            here = pl.ds(pl.multiple_of(block * 8, 8), 8)
            planes = []
            for plane in range(PLANES):
                planes.append(
                    jnp.concatenate(
                        [first[chan, plane, here, :] for chan in range(CH)]
                        + [second[chan, plane, here, :] for chan in range(CH)],
                        axis=0,
                    )
                )
            cells = jnp.concatenate([jnp.concatenate(planes, axis=1), ones_row], axis=0)
            total = dot(lin_left[:, 0:176], cells)
            for plane in range(PLANES):
                for chan in range(CH):
                    base[plane * CH + chan, here, :] = total[
                        chan * 8 : chan * 8 + 8, plane * 128 : plane * 128 + 128
                    ]

    @pl.when(ch == 0)
    def _():
        channel_map(fld, peer)

    @pl.when(ch == 1)
    def _():
        channel_map(peer, fld)

    load_w.wait()
    w_wait()
    spread_a = dot_tn(recv_w[...], fx[0])
    spread_b = dot_tn(recv_w[...], fx[1])
    coeffs = (spread_a[0:320] + spread_b[320:640]).astype(BF16).astype(F32)

    def mix(first, chan):
        total = jnp.zeros((32, M), F32)
        for i in range(CH):
            total = total + wts[i, first + chan].astype(F32) * coeffs[i * 32 : i * 32 + 32]
        return total

    for chan in range(CH):
        mix_send[chan] = mix((1 - ch) * CH, chan).astype(BF16)
    mix_copy = remote(mix_send, mix_recv, mix_sem.at[0], mix_sem.at[1], twin)
    mix_copy.start()
    own = [mix(ch * CH, chan) for chan in range(CH)]
    mix_copy.wait_recv()
    for chan in range(CH):
        value = (own[chan] + mix_recv[chan].astype(F32)).astype(BF16)
        mixed[0, chan * 32 : chan * 32 + 32, :] = value
        mixed[1, 320 + chan * 32 : 320 + chan * 32 + 32, :] = value
    send_v[...] = (dot_nt(gx[0], mixed[0]) + dot_nt(gx[1], mixed[1])).astype(BF16)
    v_start()
    v_wait()
    send_u[...] = dot_tn(perm_b[...], recv_v[...]).astype(BF16)
    u_start()

    @pl.when(pool == 1)
    def _():
        couple.wait_recv()

        @pl.loop(0, CH)
        def _(chan):
            cells = coupled_in[:, pl.ds(pl.multiple_of(chan * 128, 128), 128)]
            row, col = iota((128, 256), 0) - 4 * chan, iota((128, 256), 1)
            pick = (
                ((row == 0) & (col == 0))
                | ((row == 1) & (col == 127))
                | ((row == 2) & (col == 128))
                | ((row == 3) & (col == 255))
            )
            value = dot(cells, unpack[...]) + dot(
                coupled_in[:, CH * 128 :], jnp.where(pick, 0.25, 0.0).astype(BF16)
            )
            value = value.astype(BF16).astype(F32)
            for plane in range(PLANES):
                base[plane * CH + chan] = base[plane * CH + chan] + value[:, plane * 128 : plane * 128 + 128]

    def expand(rows, table, part):
        ordered = dot_tn(perm_a[...], rows).astype(BF16)
        for group in range(5):
            spread_left = jnp.concatenate(
                [ordered[half * 64 : half * 64 + 64, group * 128 : group * 128 + 128] for half in range(2)],
                axis=1,
            )
            value = dot(spread_left, table).astype(BF16)
            for lane in range(4):
                right[group * 4 + lane, part * 64 : part * 64 + 64, :] = value[:, lane * 128 : lane * 128 + 128]

    u_wait()
    modes_out = remote(recv_u, modes_in.at[0], modes_sem.at[0], modes_sem.at[1], other_pool)
    modes_up = remote(modes_in.at[0], modes_in.at[1], modes_sem.at[2], modes_sem.at[3], up)
    modes_down = remote(modes_in.at[0], modes_in.at[2], modes_sem.at[4], modes_sem.at[5], down)

    @pl.when(pool == 1)
    def _():
        modes_out.start()

    expand(recv_u[...], bdi[...], 0)

    @pl.when(is_coarse)
    def _():
        modes_out.wait_recv()
        modes_up.start()
        modes_down.start()
        expand(modes_in[0], bdc[...], 1)
        modes_up.wait_recv()
        expand(modes_in[1], bdc[...], 2)
        modes_down.wait_recv()
        expand(modes_in[2], bdc[...], 3)

    @pl.loop(0, PC)
    def _(pc):
        plane, chan = pc // CH, lax.rem(pc, CH)
        total = dot(left[...], right[pc]) + base[pc]
        value = total * (1.0 + lax.erf(total * np.float32(np.sqrt(0.5)))) * 0.5
        result[chan, plane] = value.astype(BF16)
        pltpu.make_async_copy(result.at[chan, plane], out.at[0, chan, plane], out_sem.at[pc]).start()

    z_sent()
    w_sent()
    v_sent()
    u_sent()
    code_up.wait_send()
    code_down.wait_send()
    to_peer.wait_send()
    mix_copy.wait_send()

    @pl.when(is_coarse)
    def _():
        near_up.wait_send()
        near_down.wait_send()
        couple.wait_send()
        modes_up.wait_send()
        modes_down.wait_send()

    @pl.when(pool == 1)
    def _():
        modes_out.wait_send()

    @pl.loop(0, PC)
    def _(pc):
        plane, chan = pc // CH, lax.rem(pc, CH)
        pltpu.make_async_copy(result.at[chan, plane], out.at[0, chan, plane], out_sem.at[pc]).wait()


def body(fields, mode_weights, lin_weights, bias, source):
    weights = jnp.swapaxes(mode_weights[0], 2, 3)
    lin = jnp.swapaxes(lin_weights[0], 0, 1)
    tables = make_tables()
    vmem = pl.BlockSpec(memory_space=pltpu.VMEM)
    anywhere = pl.BlockSpec(memory_space=pl.ANY)
    dma = pltpu.SemaphoreType.DMA
    scratch = [
        pltpu.VMEM((CH, PLANES, NY, NZ), BF16),
        pltpu.VMEM((CH, PLANES, NY, NZ), BF16),
        pltpu.VMEM((CH, 2 * CH, 32, M), BF16),
        pltpu.VMEM((320, 512), BF16),
        pltpu.VMEM((128, LANES), BF16),
        pltpu.VMEM((128, LANES), BF16),
        pltpu.VMEM((128, LANES), BF16),
        pltpu.VMEM((128, LANES), BF16),
        pltpu.VMEM((128, LANES), BF16),
        pltpu.VMEM((CH, 32, M), BF16),
        pltpu.VMEM((CH, 32, M), BF16),
        pltpu.VMEM((2, LANES, M), BF16),
        pltpu.VMEM((128, LANES), BF16),
        pltpu.VMEM((128, LANES), BF16),
        pltpu.VMEM((128, LANES), BF16),
        pltpu.VMEM((128, LANES), BF16),
        pltpu.VMEM((8, 128), F32),
        pltpu.VMEM((2, 8, 128), F32),
        pltpu.VMEM((PC, NY, NZ), F32),
        pltpu.VMEM((80, 256), BF16),
        pltpu.VMEM((NY, PACKED), BF16),
        pltpu.VMEM((128, PACKED), BF16),
        pltpu.VMEM((128, PACKED), BF16),
        pltpu.VMEM((NY, PACKED), BF16),
        pltpu.VMEM((NY, PACKED), BF16),
        pltpu.VMEM((3, 128, LANES), BF16),
        pltpu.VMEM((NY, 256), BF16),
        pltpu.VMEM((PC, 256, 128), BF16),
        pltpu.VMEM((CH, PLANES, NY, NZ), BF16),
        dma, dma,
        dma((RZ,)), dma((RZ,)), dma((RW,)), dma((RW,)), dma((RW,)), dma((RW,)), dma((RZ,)), dma((RZ,)),
        dma((2,)), dma((4,)), dma((2,)), dma((4,)), dma((2,)), dma((6,)), dma((PC,)),
    ]
    return pl.pallas_call(
        kernel,
        out_shape=jax.ShapeDtypeStruct(fields.shape, BF16),
        in_specs=[anywhere, anywhere] + [vmem] * (3 + len(tables)),
        out_specs=anywhere,
        scratch_shapes=scratch,
        compiler_params=pltpu.CompilerParams(
            collective_id=0, has_side_effects=True, vmem_limit_bytes=60 * 2**20
        ),
    )(fields, weights, lin, bias, source, *tables)


def solution(mesh):
    return jax.shard_map(
        body,
        mesh=mesh,
        in_specs=(
            P("pool", "ch", "slab", None, None),
            P("pool", "ch", None, None, "slab"),
            P("pool", None, "ch"),
            P("pool", "ch"),
            P("slab", None),
        ),
        out_specs=P("pool", "ch", "slab", None, None),
        check_vma=False,
    )
```

```python
import functools

import jax
import jax.numpy as jnp
import numpy as np
from jax import lax
from jax.experimental import pallas as pl
from jax.experimental.pallas import tpu as pltpu
from jax.sharding import PartitionSpec as P

MESH = pl.DeviceIdType.MESH
BF16 = jnp.bfloat16
F32 = jnp.float32

CH, PLANES, NY, NZ, M = 10, 2, 224, 128, 64
NX = 256
RZ, RW = 16, 8
PC = CH * PLANES
LANES = PC * 32
BLOCKS, ROWS = 8, 28
PACKED = CH * 128 + 128
NAMES = ("fy", "gy", "fx", "gx", "bdf", "bdi", "bdc", "perm_a", "perm_b", "pack", "unpack")


def dft(length):
    cells = np.arange(length, dtype=np.float32)
    order = np.arange(M, dtype=np.int32)
    half = M // 2
    freq = np.where(order < half, order, order - half + 1).astype(np.float32)
    angle = np.float32(2.0 * np.pi) * freq[:, None] * cells[None, :] / np.float32(length)
    forward = np.where((order < half)[:, None], np.cos(angle), np.sin(angle)).astype(np.float32)
    return forward, (forward.T * np.float32(2.0 / length)).astype(np.float32)


def rounded(array):
    return np.asarray(array, np.float32).astype(BF16)


def interp():
    fine = np.arange(NZ)[:, None]
    coarse = np.arange(NZ)[None, :]
    centre = NZ // 4 + fine // 2
    second = centre - 1 + 2 * (fine % 2)
    return (0.75 * (coarse == centre) + 0.25 * (coarse == second)).astype(np.float32)


def make_tables():
    fwd_x, inv_x = (rounded(table).astype(np.float32) for table in dft(NX))
    fwd_y, inv_y = (rounded(table).astype(np.float32) for table in dft(NY))
    fwd_z, inv_z = (rounded(table).astype(np.float32) for table in dft(NZ))
    mat = interp()
    inv_c = (0.5 * mat).T @ inv_z
    bdf = np.zeros((4, NZ, 2, 4, 32), np.float32)
    bdi = np.zeros((2, 4, 32, 4, NZ), np.float32)
    bdc = np.zeros((2, 4, 32, 4, NZ), np.float32)
    for group in range(4):
        for half in range(2):
            part = slice(half * 32, half * 32 + 32)
            bdf[group, :, half, group, :] = fwd_z[part].T
            bdi[half, group, :, group, :] = inv_z[:, part].T
            bdc[half, group, :, group, :] = inv_c[:, part].T
    perm_a = np.zeros((128, 128), np.float32)
    perm_b = np.zeros((128, 128), np.float32)
    for z in range(RZ):
        for w in range(RW):
            perm_a[z * 8 + w, (w % 2) * 64 + z * 4 + w // 2] = 1.0
            perm_b[w * 16 + z, z * 8 + w] = 1.0
    fx = np.zeros((2, 128, M), np.float32)
    gx = np.zeros((2, 128, M), np.float32)
    for z in range(RZ):
        for w in range(RW):
            for plane in range(2):
                cell = 2 * (z * 8 + w) + plane
                fx[plane, w * 16 + z] = fwd_x[:, cell]
                gx[plane, w * 16 + z] = inv_x[cell]
    pack = np.zeros((2, NZ, 128), np.float32)
    unpack = np.zeros((128, 2, NZ), np.float32)
    for plane in range(2):
        for cell in range(64):
            pack[plane, 32 + cell, plane * 64 + cell] = 1.0
            unpack[plane * 64 + cell, plane, :] = mat[:, 32 + cell]
    values = {
        "fy": fwd_y,
        "gy": inv_y,
        "fx": fx,
        "gx": gx,
        "bdf": bdf.reshape(512, 256),
        "bdi": bdi.reshape(256, 512),
        "bdc": bdc.reshape(256, 512),
        "perm_a": perm_a,
        "perm_b": perm_b,
        "pack": pack.reshape(256, 128),
        "unpack": unpack.reshape(128, 256),
    }
    return [rounded(values[name]) for name in NAMES]


def dot(left, right):
    return lax.dot_general(left, right, (((1,), (0,)), ((), ())), preferred_element_type=F32)


def dot_nt(left, right):
    return lax.dot_general(left, right, (((1,), (1,)), ((), ())), preferred_element_type=F32)


def dot_tn(left, right):
    return lax.dot_general(left, right, (((0,), (0,)), ((), ())), preferred_element_type=F32)


def iota(shape, axis):
    return lax.broadcasted_iota(jnp.int32, shape, axis)


def hot(mask):
    return jnp.where(mask, 1.0, 0.0)


def kernel(
    field, weights, lin, bias, source,
    fy, gy, fx, gx, bdf, bdi, bdc, perm_a, perm_b, pack, unpack,
    out,
    fld, peer, wts, along, rows_a, send_z, recv_z, send_w, recv_w, mix_send, mix_recv, mixed,
    send_v, recv_v, send_u, recv_u, codes, codes_in, base, lin_left, packed, near_send, near_recv,
    coupled, coupled_in, modes_in, left, right, result,
    load_sem, wts_sem, z_send, z_recv, w_send, w_recv, v_send, v_recv, u_send, u_recv,
    peer_sem, code_sem, mix_sem, near_sem, couple_sem,
    out_send, out_recv, up_send, up_recv, down_send, down_recv, out_sem,
):
    pool = lax.axis_index("pool")
    slab = lax.axis_index("slab")
    ch = lax.axis_index("ch")
    zed, wid = slab // RW, lax.rem(slab, RW)
    count = RZ * RW
    above, below = lax.rem(slab + 1, count), lax.rem(slab + count - 1, count)
    is_coarse = pool == 0
    has_up, has_down = slab < count - 1, slab > 0

    def at_z(target):
        return (pool, target * RW + wid, ch)

    def at_w(target):
        return (pool, zed * RW + target, ch)

    twin = (pool, slab, 1 - ch)
    other_pool = (1 - pool, slab, ch)
    up, down = (pool, above, ch), (pool, below, ch)

    def remote(src, dst, send, recv, device):
        return pltpu.make_async_remote_copy(
            src_ref=src, dst_ref=dst, send_sem=send, recv_sem=recv, device_id=device, device_id_type=MESH
        )

    barrier = pltpu.get_barrier_semaphore()

    def greet(device):
        pl.semaphore_signal(barrier, inc=1, device_id=device, device_id_type=MESH)

    load = pltpu.make_async_copy(field.at[0], fld, load_sem)
    load.start()
    load_w = pltpu.make_async_copy(weights, wts, wts_sem)
    load_w.start()

    @pl.loop(1, RZ)
    def _(step):
        greet(at_z(lax.rem(zed + step, RZ)))

    @pl.loop(1, RW)
    def _(step):
        greet(at_w(lax.rem(wid + step, RW)))

    greet(twin)
    greet(other_pool)

    @pl.when(has_up)
    def _():
        greet(up)

    @pl.when(has_down)
    def _():
        greet(down)

    @pl.when(slab == 0)
    def _():
        codes_in[0] = jnp.full((8, 128), -1.0, F32)
        near_recv[0:64] = jnp.zeros((64, PACKED), BF16)
        modes_in[1] = jnp.zeros((128, LANES), BF16)

    @pl.when(slab == count - 1)
    def _():
        codes_in[1] = jnp.full((8, 128), -1.0, F32)
        near_recv[64:128] = jnp.zeros((64, PACKED), BF16)
        modes_in[2] = jnp.zeros((128, LANES), BF16)

    listed = source[...]
    lower = hot((listed == slab - 1) & (listed >= 0))
    upper = hot(listed == slab + 1)
    same = hot(listed == slab)
    before = hot(iota((BLOCKS, BLOCKS), 0) < iota((BLOCKS, BLOCKS), 1))
    lower_rank = dot(lower.astype(BF16), before.astype(BF16))
    upper_rank = dot(upper.astype(BF16), before.astype(BF16))
    codes[...] = jnp.full(codes.shape, -1.0, F32)
    codes[0:1, 0:BLOCKS] = jnp.where(lower > 0.5, lower_rank, -1.0)
    codes[1:2, 0:BLOCKS] = jnp.where(upper > 0.5, upper_rank, -1.0)
    codes[2:3, 0:BLOCKS] = same - 1.0

    spread = dot(
        lin[...], hot((iota((2 * CH, 256), 1) // 8) == iota((2 * CH, 256), 0)).astype(BF16)
    )
    shift = dot_tn(
        jnp.broadcast_to(bias[...], (8, CH)),
        hot((iota((8, 256), 0) == 0) & (iota((8, 256), 1) == 160)).astype(BF16),
    )
    per_row = dot(
        hot((iota((80, CH), 0) // 8) == iota((80, CH), 1)).astype(BF16), (spread + shift).astype(BF16)
    )
    keep = (lax.rem(iota((80, 256), 0), 8) == lax.rem(iota((80, 256), 1), 8)) | (
        iota((80, 256), 1) == 160
    )
    lin_left[...] = jnp.where(keep, per_row, 0.0).astype(BF16)

    load.wait()
    for pc in range(PC):
        plane, chan = pc // CH, pc % CH
        part = dot(fy[...], fld[chan, plane])
        group, lane = pc // 4, pc % 4
        along[group * 64 : group * 64 + 64, lane * 128 : lane * 128 + 128] = part.astype(BF16)
    along_z = dot(along[...], bdf[...]).astype(BF16)
    for group in range(5):
        for half in range(2):
            rows_a[half * 64 : half * 64 + 64, group * 128 : group * 128 + 128] = along_z[
                group * 64 : group * 64 + 64, half * 128 : half * 128 + 128
            ]
    send_z[...] = dot(perm_a[...], rows_a[...]).astype(BF16)

    pl.semaphore_wait(barrier, RZ - 1 + RW - 1 + 2 + has_up.astype(jnp.int32) + has_down.astype(jnp.int32))

    def neighbours(upward, downward):
        def start():
            @pl.when(has_up)
            def _():
                upward.start()

            @pl.when(has_down)
            def _():
                downward.start()

        def wait_recv():
            @pl.when(has_down)
            def _():
                upward.wait_recv()

            @pl.when(has_up)
            def _():
                downward.wait_recv()

        def wait_send():
            @pl.when(has_up)
            def _():
                upward.wait_send()

            @pl.when(has_down)
            def _():
                downward.wait_send()

        return start, wait_recv, wait_send

    def exchange(size, mine, rows, device, src, dst, send, recv):
        def piece(ref, index):
            return ref.at[pl.ds(pl.multiple_of(index * rows, rows), rows), :]

        def copy(step):
            middle = (step + 1) // 2
            apart = size // 2 + middle * (1 - 2 * lax.rem(step, 2))
            target = lax.rem(mine + apart, size)
            return remote(piece(src, target), piece(dst, mine), send.at[target], recv.at[mine], device(target))

        def from_origin(origin):
            return remote(piece(src, origin), piece(dst, origin), send.at[origin], recv.at[origin], device(origin))

        def start():
            @pl.loop(0, size - 1)
            def _(step):
                copy(step).start()

            here = pl.ds(pl.multiple_of(mine * rows, rows), rows)
            dst[here, :] = src[here, :]

        def wait_recv():
            @pl.loop(0, size - 1)
            def _(step):
                from_origin(lax.rem(mine + step + 1, size)).wait_recv()

        def wait_send():
            @pl.loop(0, size - 1)
            def _(step):
                from_origin(lax.rem(mine + step + 1, size)).wait_send()

        return start, wait_recv, wait_send, from_origin

    z_start, z_wait, z_sent, _ = exchange(RZ, zed, 8, at_z, send_z, recv_z, z_send, z_recv)
    w_start, w_wait, w_sent, _ = exchange(RW, wid, 16, at_w, send_w, recv_w, w_send, w_recv)
    v_start, v_wait, v_sent, _ = exchange(RW, wid, 16, at_w, send_v, recv_v, v_send, v_recv)
    u_start, _, u_sent, u_from = exchange(RZ, zed, 8, at_z, send_u, recv_u, u_send, u_recv)

    z_start()
    code_start, code_wait, code_sent = neighbours(
        remote(codes, codes_in.at[0], code_sem.at[0], code_sem.at[1], up),
        remote(codes, codes_in.at[1], code_sem.at[2], code_sem.at[3], down),
    )
    code_start()
    to_peer = remote(fld, peer, peer_sem.at[0], peer_sem.at[1], twin)
    to_peer.start()

    near_start, near_wait, near_sent = neighbours(
        remote(near_send.at[0:64], near_recv.at[0:64], near_sem.at[0], near_sem.at[1], up),
        remote(near_send.at[64:128], near_recv.at[64:128], near_sem.at[2], near_sem.at[3], down),
    )
    couple = remote(coupled, coupled_in, couple_sem.at[0], couple_sem.at[1], other_pool)

    @pl.when(is_coarse)
    def _():
        edges = jnp.zeros((NY, 128), F32)
        for chan in range(CH):
            pair = jnp.concatenate([fld[chan, 0], fld[chan, 1]], axis=1)
            packed[:, chan * 128 : chan * 128 + 128] = dot(pair, pack[...]).astype(BF16)
            row, col = iota((256, 128), 0), iota((256, 128), 1) - 4 * chan
            pick = (
                ((row == 31) & (col == 0))
                | ((row == 96) & (col == 1))
                | ((row == 128 + 31) & (col == 2))
                | ((row == 128 + 96) & (col == 3))
            )
            edges = edges + dot(pair, hot(pick).astype(BF16))
        packed[:, CH * 128 :] = edges.astype(BF16)

    code_wait()
    from_below, from_above = codes_in[0], codes_in[1]

    def block_columns(code):
        table = hot(iota((8, NY), 1) // ROWS == iota((8, NY), 0)).astype(BF16)
        return dot(code[:, 0:BLOCKS].astype(BF16), table)

    def block_rows(code):
        table = hot(iota((NY, 8), 0) // ROWS == iota((NY, 8), 1)).astype(BF16)
        return dot_nt(table, code[:, 0:BLOCKS].astype(BF16))

    own_rows = block_rows(codes[...])

    @pl.when(is_coarse)
    def _():
        for part, row in ((0, block_columns(from_above)[0:1]), (1, block_columns(from_below)[1:2])):
            slot, cell = iota((64, NY), 0), iota((64, NY), 1)
            pick = ((slot // ROWS).astype(F32) == row) & (lax.rem(slot, ROWS) == lax.rem(cell, ROWS))
            chosen = dot(hot(pick).astype(BF16), packed[...])
            near_send[part * 64 : part * 64 + 64, :] = chosen.astype(BF16)
        near_start()

    below_rows, above_rows = block_rows(from_below), block_rows(from_above)
    gy_all = gy[...].astype(F32)
    coarse_scale = jnp.where(is_coarse, 1.0, 0.0)
    left[:, 0:64] = gy[...]
    for part, mask in (
        (1, own_rows[:, 2:3]),
        (2, below_rows[:, 1:2]),
        (3, above_rows[:, 0:1]),
    ):
        left[:, part * 64 : part * 64 + 64] = (gy_all * (hot(mask > -0.5) * coarse_scale)).astype(BF16)
    right[...] = jnp.zeros(right.shape, BF16)
    mixed[...] = jnp.zeros(mixed.shape, BF16)

    z_wait()
    send_w[...] = dot(perm_b[...], recv_z[...]).astype(BF16)
    w_start()

    @pl.when(is_coarse)
    def _():
        near_wait()
        slot, cell = iota((NY, 128), 1), iota((NY, 128), 0)
        code = jnp.where(slot < 64, own_rows[:, 0:1], own_rows[:, 1:2])
        inner = lax.rem(slot, 64)
        pick = ((inner // ROWS).astype(F32) == code) & (lax.rem(inner, ROWS) == lax.rem(cell, ROWS))
        moved = dot(hot(pick).astype(BF16), near_recv[...])
        kept = hot(own_rows[:, 2:3] > -0.5)
        coupled[...] = (moved + packed[...].astype(F32) * kept).astype(BF16)
        couple.start()

    to_peer.wait_recv()
    ones_row = hot(iota((16, 256), 0) == 0).astype(BF16)

    def channel_map(first, second):
        @pl.loop(0, NY // 8)
        def _(block):
            here = pl.ds(pl.multiple_of(block * 8, 8), 8)
            planes = []
            for plane in range(PLANES):
                planes.append(
                    jnp.concatenate(
                        [first[chan, plane, here, :] for chan in range(CH)]
                        + [second[chan, plane, here, :] for chan in range(CH)],
                        axis=0,
                    )
                )
            cells = jnp.concatenate([jnp.concatenate(planes, axis=1), ones_row], axis=0)
            total = dot(lin_left[:, 0:176], cells)
            for plane in range(PLANES):
                for chan in range(CH):
                    base[plane * CH + chan, here, :] = total[
                        chan * 8 : chan * 8 + 8, plane * 128 : plane * 128 + 128
                    ]

    @pl.when(ch == 0)
    def _():
        channel_map(fld, peer)

    @pl.when(ch == 1)
    def _():
        channel_map(peer, fld)

    load_w.wait()
    w_wait()
    spread_a = dot_tn(recv_w[...], fx[0])
    spread_b = dot_tn(recv_w[...], fx[1])
    coeffs = (spread_a[0:320] + spread_b[320:640]).astype(BF16).astype(F32)

    def mix(first, chan):
        total = jnp.zeros((32, M), F32)
        for i in range(CH):
            total = total + wts[i, first + chan].astype(F32) * coeffs[i * 32 : i * 32 + 32]
        return total

    for chan in range(CH):
        mix_send[chan] = mix((1 - ch) * CH, chan).astype(BF16)
    mix_copy = remote(mix_send, mix_recv, mix_sem.at[0], mix_sem.at[1], twin)
    mix_copy.start()
    own = [mix(ch * CH, chan) for chan in range(CH)]
    mix_copy.wait_recv()
    for chan in range(CH):
        value = (own[chan] + mix_recv[chan].astype(F32)).astype(BF16)
        mixed[0, chan * 32 : chan * 32 + 32, :] = value
        mixed[1, 320 + chan * 32 : 320 + chan * 32 + 32, :] = value
    send_v[...] = (dot_nt(gx[0], mixed[0]) + dot_nt(gx[1], mixed[1])).astype(BF16)
    v_start()
    v_wait()
    send_u[...] = dot_tn(perm_b[...], recv_v[...]).astype(BF16)
    u_start()

    @pl.when(pool == 1)
    def _():
        couple.wait_recv()

        @pl.loop(0, CH)
        def _(chan):
            cells = coupled_in[:, pl.ds(pl.multiple_of(chan * 128, 128), 128)]
            row, col = iota((128, 256), 0) - 4 * chan, iota((128, 256), 1)
            pick = (
                ((row == 0) & (col == 0))
                | ((row == 1) & (col == 127))
                | ((row == 2) & (col == 128))
                | ((row == 3) & (col == 255))
            )
            value = dot(cells, unpack[...]) + dot(
                coupled_in[:, CH * 128 :], jnp.where(pick, 0.25, 0.0).astype(BF16)
            )
            value = value.astype(BF16).astype(F32)
            for plane in range(PLANES):
                base[plane * CH + chan] = base[plane * CH + chan] + value[:, plane * 128 : plane * 128 + 128]

    def expand(rows, table, part):
        ordered = dot_tn(perm_a[...], rows).astype(BF16)
        for group in range(5):
            spread_left = jnp.concatenate(
                [ordered[half * 64 : half * 64 + 64, group * 128 : group * 128 + 128] for half in range(2)],
                axis=1,
            )
            value = dot(spread_left, table).astype(BF16)
            for lane in range(4):
                right[group * 4 + lane, part * 64 : part * 64 + 64, :] = value[:, lane * 128 : lane * 128 + 128]

    def near_first(step):
        apart = ((step + 1) // 2) * (1 - 2 * lax.rem(step, 2))
        return lax.rem(zed + apart + RZ, RZ)

    def chunk(ref, index):
        return ref.at[pl.ds(pl.multiple_of(index * 8, 8), 8), :]

    def modes_out(origin):
        return remote(
            chunk(recv_u, origin), chunk(modes_in.at[0], origin), out_send.at[origin], out_recv.at[origin], other_pool
        )

    def modes_near(origin):
        source_ref = chunk(modes_in.at[0], origin)
        return neighbours(
            remote(source_ref, chunk(modes_in.at[1], origin), up_send.at[origin], up_recv.at[origin], up),
            remote(source_ref, chunk(modes_in.at[2], origin), down_send.at[origin], down_recv.at[origin], down),
        )

    @pl.loop(0, RZ)
    def _(step):
        origin = near_first(step)

        @pl.when(origin != zed)
        def _():
            u_from(origin).wait_recv()

        @pl.when(pool == 1)
        def _():
            modes_out(origin).start()

        @pl.when(is_coarse)
        def _():
            modes_out(origin).wait_recv()
            modes_near(origin)[0]()

    expand(recv_u[...], bdi[...], 0)

    @pl.when(is_coarse)
    def _():
        expand(modes_in[0], bdc[...], 1)

        @pl.loop(0, RZ)
        def _(step):
            modes_near(near_first(step))[1]()

        expand(modes_in[1], bdc[...], 2)
        expand(modes_in[2], bdc[...], 3)

    @pl.loop(0, PC)
    def _(pc):
        plane, chan = pc // CH, lax.rem(pc, CH)
        total = dot(left[...], right[pc]) + base[pc]
        value = total * (1.0 + lax.erf(total * np.float32(np.sqrt(0.5)))) * 0.5
        result[chan, plane] = value.astype(BF16)
        pltpu.make_async_copy(result.at[chan, plane], out.at[0, chan, plane], out_sem.at[pc]).start()

    z_sent()
    w_sent()
    v_sent()
    u_sent()
    code_sent()
    to_peer.wait_send()
    mix_copy.wait_send()

    @pl.when(is_coarse)
    def _():
        near_sent()
        couple.wait_send()

        @pl.loop(0, RZ)
        def _(step):
            modes_near(near_first(step))[2]()

    @pl.when(pool == 1)
    def _():
        @pl.loop(0, RZ)
        def _(step):
            modes_out(near_first(step)).wait_send()

    @pl.loop(0, PC)
    def _(pc):
        plane, chan = pc // CH, lax.rem(pc, CH)
        pltpu.make_async_copy(result.at[chan, plane], out.at[0, chan, plane], out_sem.at[pc]).wait()


def body(fields, mode_weights, lin_weights, bias, source):
    weights = jnp.swapaxes(mode_weights[0], 2, 3)
    lin = jnp.swapaxes(lin_weights[0], 0, 1)
    tables = make_tables()
    vmem = pl.BlockSpec(memory_space=pltpu.VMEM)
    anywhere = pl.BlockSpec(memory_space=pl.ANY)
    dma = pltpu.SemaphoreType.DMA
    scratch = [
        pltpu.VMEM((CH, PLANES, NY, NZ), BF16),
        pltpu.VMEM((CH, PLANES, NY, NZ), BF16),
        pltpu.VMEM((CH, 2 * CH, 32, M), BF16),
        pltpu.VMEM((320, 512), BF16),
        pltpu.VMEM((128, LANES), BF16),
        pltpu.VMEM((128, LANES), BF16),
        pltpu.VMEM((128, LANES), BF16),
        pltpu.VMEM((128, LANES), BF16),
        pltpu.VMEM((128, LANES), BF16),
        pltpu.VMEM((CH, 32, M), BF16),
        pltpu.VMEM((CH, 32, M), BF16),
        pltpu.VMEM((2, LANES, M), BF16),
        pltpu.VMEM((128, LANES), BF16),
        pltpu.VMEM((128, LANES), BF16),
        pltpu.VMEM((128, LANES), BF16),
        pltpu.VMEM((128, LANES), BF16),
        pltpu.VMEM((8, 128), F32),
        pltpu.VMEM((2, 8, 128), F32),
        pltpu.VMEM((PC, NY, NZ), F32),
        pltpu.VMEM((80, 256), BF16),
        pltpu.VMEM((NY, PACKED), BF16),
        pltpu.VMEM((128, PACKED), BF16),
        pltpu.VMEM((128, PACKED), BF16),
        pltpu.VMEM((NY, PACKED), BF16),
        pltpu.VMEM((NY, PACKED), BF16),
        pltpu.VMEM((3, 128, LANES), BF16),
        pltpu.VMEM((NY, 256), BF16),
        pltpu.VMEM((PC, 256, 128), BF16),
        pltpu.VMEM((CH, PLANES, NY, NZ), BF16),
        dma, dma,
        dma((RZ,)), dma((RZ,)), dma((RW,)), dma((RW,)), dma((RW,)), dma((RW,)), dma((RZ,)), dma((RZ,)),
        dma((2,)), dma((4,)), dma((2,)), dma((4,)), dma((2,)),
        dma((RZ,)), dma((RZ,)), dma((RZ,)), dma((RZ,)), dma((RZ,)), dma((RZ,)), dma((PC,)),
    ]
    return pl.pallas_call(
        kernel,
        out_shape=jax.ShapeDtypeStruct(fields.shape, BF16),
        in_specs=[anywhere, anywhere] + [vmem] * (3 + len(tables)),
        out_specs=anywhere,
        scratch_shapes=scratch,
        compiler_params=pltpu.CompilerParams(
            collective_id=0, has_side_effects=True, vmem_limit_bytes=60 * 2**20
        ),
    )(fields, weights, lin, bias, source, *tables)


def solution(mesh):
    return jax.shard_map(
        body,
        mesh=mesh,
        in_specs=(
            P("pool", "ch", "slab", None, None),
            P("pool", "ch", None, None, "slab"),
            P("pool", None, "ch"),
            P("pool", "ch"),
            P("slab", None),
        ),
        out_specs=P("pool", "ch", "slab", None, None),
        check_vma=False,
    )
```

```python
import functools

import jax
import jax.numpy as jnp
import numpy as np
from jax import lax
from jax.experimental import pallas as pl
from jax.experimental.pallas import tpu as pltpu
from jax.sharding import PartitionSpec as P

MESH = pl.DeviceIdType.MESH
BF16 = jnp.bfloat16
F32 = jnp.float32

CH, PLANES, NY, NZ, M = 10, 2, 224, 128, 64
NX = 256
RZ, RW = 16, 8
PC = CH * PLANES
LANES = PC * 32
BLOCKS, ROWS = 8, 28
PACKED = CH * 128 + 128
LATE, MIDDLE = 8, 3
NAMES = ("fy", "bdf", "perm_a", "perm_b", "pack", "gy", "fx", "gx", "bdi", "bdc", "unpack")


def dft(length):
    cells = np.arange(length, dtype=np.float32)
    order = np.arange(M, dtype=np.int32)
    half = M // 2
    freq = np.where(order < half, order, order - half + 1).astype(np.float32)
    angle = np.float32(2.0 * np.pi) * freq[:, None] * cells[None, :] / np.float32(length)
    forward = np.where((order < half)[:, None], np.cos(angle), np.sin(angle)).astype(np.float32)
    return forward, (forward.T * np.float32(2.0 / length)).astype(np.float32)


def rounded(array):
    return np.asarray(array, np.float32).astype(BF16)


def interp():
    fine = np.arange(NZ)[:, None]
    coarse = np.arange(NZ)[None, :]
    centre = NZ // 4 + fine // 2
    second = centre - 1 + 2 * (fine % 2)
    return (0.75 * (coarse == centre) + 0.25 * (coarse == second)).astype(np.float32)


def make_tables():
    fwd_x, inv_x = (rounded(table).astype(np.float32) for table in dft(NX))
    fwd_y, inv_y = (rounded(table).astype(np.float32) for table in dft(NY))
    fwd_z, inv_z = (rounded(table).astype(np.float32) for table in dft(NZ))
    mat = interp()
    inv_c = (0.5 * mat).T @ inv_z
    bdf = np.zeros((4, NZ, 2, 4, 32), np.float32)
    bdi = np.zeros((2, 4, 32, 4, NZ), np.float32)
    bdc = np.zeros((2, 4, 32, 4, NZ), np.float32)
    for group in range(4):
        for half in range(2):
            part = slice(half * 32, half * 32 + 32)
            bdf[group, :, half, group, :] = fwd_z[part].T
            bdi[half, group, :, group, :] = inv_z[:, part].T
            bdc[half, group, :, group, :] = inv_c[:, part].T
    perm_a = np.zeros((128, 128), np.float32)
    perm_b = np.zeros((128, 128), np.float32)
    for z in range(RZ):
        for w in range(RW):
            perm_a[z * 8 + w, (w % 2) * 64 + z * 4 + w // 2] = 1.0
            perm_b[w * 16 + z, z * 8 + w] = 1.0
    fx = np.zeros((2, 128, M), np.float32)
    gx = np.zeros((2, 128, M), np.float32)
    for z in range(RZ):
        for w in range(RW):
            for plane in range(2):
                cell = 2 * (z * 8 + w) + plane
                fx[plane, w * 16 + z] = fwd_x[:, cell]
                gx[plane, w * 16 + z] = inv_x[cell]
    pack = np.zeros((2, NZ, 128), np.float32)
    unpack = np.zeros((128, 2, NZ), np.float32)
    for plane in range(2):
        for cell in range(64):
            pack[plane, 32 + cell, plane * 64 + cell] = 1.0
            unpack[plane * 64 + cell, plane, :] = mat[:, 32 + cell]
    values = {
        "fy": fwd_y,
        "gy": inv_y,
        "fx": fx,
        "gx": gx,
        "bdf": bdf.reshape(512, 256),
        "bdi": bdi.reshape(256, 512),
        "bdc": bdc.reshape(256, 512),
        "perm_a": perm_a,
        "perm_b": perm_b,
        "pack": pack.reshape(256, 128),
        "unpack": unpack.reshape(128, 256),
    }
    return [rounded(values[name]) for name in NAMES]


def dot(left, right):
    return lax.dot_general(left, right, (((1,), (0,)), ((), ())), preferred_element_type=F32)


def dot_nt(left, right):
    return lax.dot_general(left, right, (((1,), (1,)), ((), ())), preferred_element_type=F32)


def dot_tn(left, right):
    return lax.dot_general(left, right, (((0,), (0,)), ((), ())), preferred_element_type=F32)


def iota(shape, axis):
    return lax.broadcasted_iota(jnp.int32, shape, axis)


def hot(mask):
    return jnp.where(mask, 1.0, 0.0)


def kernel(
    field, weights, lin_hbm, bias_hbm, source_hbm, *rest,
):
    tables, (out, lin, bias, source), rest = rest[: len(NAMES)], rest[len(NAMES) : len(NAMES) + 4], rest[len(NAMES) + 4 :]
    run(field, weights, lin_hbm, bias_hbm, source_hbm, tables, out, lin, bias, source, rest[: len(NAMES)], *rest)


def run(
    field, weights, lin_hbm, bias_hbm, source_hbm, tables_hbm, out, lin, bias, source, tables,
    fy, bdf, perm_a, perm_b, pack, gy, fx, gx, bdi, bdc, unpack,
    fld, peer, wts, along, rows_a, send_z, recv_z, send_w, recv_w, mix_send, mix_recv, mixed,
    send_v, recv_v, send_u, recv_u, codes, codes_in, base, lin_left, packed, near_send, near_recv,
    coupled, coupled_in, modes_in, left, right, result,
    load_sem, wts_sem, z_send, z_recv, w_send, w_recv, v_send, v_recv, u_send, u_recv,
    peer_sem, code_sem, mix_sem, near_sem, couple_send, couple_recv, table_sem,
    out_send, out_recv, up_send, up_recv, down_send, down_recv, out_sem,
):
    pool = lax.axis_index("pool")
    slab = lax.axis_index("slab")
    ch = lax.axis_index("ch")
    zed, wid = slab // RW, lax.rem(slab, RW)
    count = RZ * RW
    above, below = lax.rem(slab + 1, count), lax.rem(slab + count - 1, count)
    is_coarse = pool == 0
    has_up, has_down = slab < count - 1, slab > 0

    def at_z(target):
        return (pool, target * RW + wid, ch)

    def at_w(target):
        return (pool, zed * RW + target, ch)

    twin = (pool, slab, 1 - ch)
    other_pool = (1 - pool, slab, ch)
    up, down = (pool, above, ch), (pool, below, ch)

    def remote(src, dst, send, recv, device):
        return pltpu.make_async_remote_copy(
            src_ref=src, dst_ref=dst, send_sem=send, recv_sem=recv, device_id=device, device_id_type=MESH
        )

    barrier = pltpu.get_barrier_semaphore()

    def greet(device):
        pl.semaphore_signal(barrier, inc=1, device_id=device, device_id_type=MESH)

    @pl.loop(0, RZ - 1)
    def _(step):
        apart = RZ // 2 + ((step + 1) // 2) * (1 - 2 * lax.rem(step, 2))
        greet(at_z(lax.rem(zed + apart, RZ)))

    @pl.loop(1, RW)
    def _(step):
        greet(at_w(lax.rem(wid + step, RW)))

    greet(twin)
    greet(other_pool)

    @pl.when(has_up)
    def _():
        greet(up)

    @pl.when(has_down)
    def _():
        greet(down)

    load = pltpu.make_async_copy(field.at[0], fld, load_sem)
    load.start()
    loads = {
        name: pltpu.make_async_copy(src, dst, table_sem.at[index])
        for index, (name, src, dst) in enumerate(
            zip(
                NAMES + ("lin", "bias", "source"),
                tuple(tables_hbm) + (lin_hbm, bias_hbm, source_hbm),
                tuple(tables) + (lin, bias, source),
            )
        )
    }
    for name in NAMES[:3]:
        loads[name].start()
    load_w = pltpu.make_async_copy(weights, wts, wts_sem)

    @pl.when(slab == 0)
    def _():
        codes_in[0] = jnp.full((8, 128), -1.0, F32)
        near_recv[0:64] = jnp.zeros((64, PACKED), BF16)
        modes_in[1] = jnp.zeros((128, LANES), BF16)

    @pl.when(slab == count - 1)
    def _():
        codes_in[1] = jnp.full((8, 128), -1.0, F32)
        near_recv[64:128] = jnp.zeros((64, PACKED), BF16)
        modes_in[2] = jnp.zeros((128, LANES), BF16)

    loads["fy"].wait()
    load.wait()
    for name in NAMES[3:] + ("lin", "bias", "source"):
        loads[name].start()
    load_w.start()
    for pc in range(PC):
        plane, chan = pc // CH, pc % CH
        part = dot(fy[...], fld[chan, plane])
        group, lane = pc // 4, pc % 4
        along[group * 64 : group * 64 + 64, lane * 128 : lane * 128 + 128] = part.astype(BF16)
    loads["bdf"].wait()
    along_z = dot(along[...], bdf[...]).astype(BF16)
    for group in range(5):
        for half in range(2):
            rows_a[half * 64 : half * 64 + 64, group * 128 : group * 128 + 128] = along_z[
                group * 64 : group * 64 + 64, half * 128 : half * 128 + 128
            ]
    loads["perm_a"].wait()
    send_z[...] = dot(perm_a[...], rows_a[...]).astype(BF16)

    pl.semaphore_wait(barrier, RZ - 1 + RW - 1 + 2 + has_up.astype(jnp.int32) + has_down.astype(jnp.int32))

    def neighbours(upward, downward):
        def start():
            @pl.when(has_up)
            def _():
                upward.start()

            @pl.when(has_down)
            def _():
                downward.start()

        def wait_recv():
            @pl.when(has_down)
            def _():
                upward.wait_recv()

            @pl.when(has_up)
            def _():
                downward.wait_recv()

        def wait_send():
            @pl.when(has_up)
            def _():
                upward.wait_send()

            @pl.when(has_down)
            def _():
                downward.wait_send()

        return start, wait_recv, wait_send

    def exchange(size, mine, rows, device, src, dst, send, recv):
        def piece(ref, index):
            return ref.at[pl.ds(pl.multiple_of(index * rows, rows), rows), :]

        def copy(step):
            middle = (step + 1) // 2
            apart = size // 2 + middle * (1 - 2 * lax.rem(step, 2))
            target = lax.rem(mine + apart, size)
            return remote(piece(src, target), piece(dst, mine), send.at[target], recv.at[mine], device(target))

        def from_origin(origin):
            return remote(piece(src, origin), piece(dst, origin), send.at[origin], recv.at[origin], device(origin))

        def start():
            @pl.loop(0, size - 1)
            def _(step):
                copy(step).start()

            here = pl.ds(pl.multiple_of(mine * rows, rows), rows)
            dst[here, :] = src[here, :]

        def wait_recv():
            @pl.loop(0, size - 1)
            def _(step):
                from_origin(lax.rem(mine + step + 1, size)).wait_recv()

        def wait_send():
            @pl.loop(0, size - 1)
            def _(step):
                from_origin(lax.rem(mine + step + 1, size)).wait_send()

        return start, wait_recv, wait_send, from_origin

    z_start, z_wait, z_sent, _ = exchange(RZ, zed, 8, at_z, send_z, recv_z, z_send, z_recv)
    w_start, w_wait, w_sent, _ = exchange(RW, wid, 16, at_w, send_w, recv_w, w_send, w_recv)
    v_start, v_wait, v_sent, _ = exchange(RW, wid, 16, at_w, send_v, recv_v, v_send, v_recv)
    u_start, _, u_sent, u_from = exchange(RZ, zed, 8, at_z, send_u, recv_u, u_send, u_recv)

    z_start()
    to_peer = remote(fld, peer, peer_sem.at[0], peer_sem.at[1], twin)
    to_peer.start()
    for name in NAMES[3:] + ("lin", "bias", "source"):
        loads[name].wait()

    listed = source[...]
    lower = hot((listed == slab - 1) & (listed >= 0))
    upper = hot(listed == slab + 1)
    same = hot(listed == slab)
    before = hot(iota((BLOCKS, BLOCKS), 0) < iota((BLOCKS, BLOCKS), 1))
    lower_rank = dot(lower.astype(BF16), before.astype(BF16))
    upper_rank = dot(upper.astype(BF16), before.astype(BF16))
    codes[...] = jnp.full(codes.shape, -1.0, F32)
    codes[0:1, 0:BLOCKS] = jnp.where(lower > 0.5, lower_rank, -1.0)
    codes[1:2, 0:BLOCKS] = jnp.where(upper > 0.5, upper_rank, -1.0)
    codes[2:3, 0:BLOCKS] = same - 1.0

    code_start, code_wait, code_sent = neighbours(
        remote(codes, codes_in.at[0], code_sem.at[0], code_sem.at[1], up),
        remote(codes, codes_in.at[1], code_sem.at[2], code_sem.at[3], down),
    )
    code_start()

    near_start, near_wait, near_sent = neighbours(
        remote(near_send.at[0:64], near_recv.at[0:64], near_sem.at[0], near_sem.at[1], up),
        remote(near_send.at[64:128], near_recv.at[64:128], near_sem.at[2], near_sem.at[3], down),
    )

    def couple(piece):
        return remote(
            coupled.at[piece], coupled_in.at[piece], couple_send.at[piece], couple_recv.at[piece], other_pool
        )


    @pl.when(is_coarse)
    def _():
        edges = jnp.zeros((NY, 128), F32)
        for chan in range(CH):
            pair = jnp.concatenate([fld[chan, 0], fld[chan, 1]], axis=1)
            packed[:, chan * 128 : chan * 128 + 128] = dot(pair, pack[...]).astype(BF16)
            row, col = iota((256, 128), 0), iota((256, 128), 1) - 4 * chan
            pick = (
                ((row == 31) & (col == 0))
                | ((row == 96) & (col == 1))
                | ((row == 128 + 31) & (col == 2))
                | ((row == 128 + 96) & (col == 3))
            )
            edges = edges + dot(pair, hot(pick).astype(BF16))
        packed[:, CH * 128 :] = edges.astype(BF16)

    code_wait()
    from_below, from_above = codes_in[0], codes_in[1]

    def block_columns(code):
        table = hot(iota((8, NY), 1) // ROWS == iota((8, NY), 0)).astype(BF16)
        return dot(code[:, 0:BLOCKS].astype(BF16), table)

    def block_rows(code):
        table = hot(iota((NY, 8), 0) // ROWS == iota((NY, 8), 1)).astype(BF16)
        return dot_nt(table, code[:, 0:BLOCKS].astype(BF16))

    own_rows = block_rows(codes[...])

    @pl.when(is_coarse)
    def _():
        for part, row in ((0, block_columns(from_above)[0:1]), (1, block_columns(from_below)[1:2])):
            slot, cell = iota((64, NY), 0), iota((64, NY), 1)
            pick = ((slot // ROWS).astype(F32) == row) & (lax.rem(slot, ROWS) == lax.rem(cell, ROWS))
            chosen = dot(hot(pick).astype(BF16), packed[...])
            near_send[part * 64 : part * 64 + 64, :] = chosen.astype(BF16)
        near_start()

    spread = dot(
        lin[...], hot((iota((2 * CH, 256), 1) // 8) == iota((2 * CH, 256), 0)).astype(BF16)
    )
    shift = dot_tn(
        jnp.broadcast_to(bias[...], (8, CH)),
        hot((iota((8, 256), 0) == 0) & (iota((8, 256), 1) == 160)).astype(BF16),
    )
    per_row = dot(
        hot((iota((80, CH), 0) // 8) == iota((80, CH), 1)).astype(BF16), (spread + shift).astype(BF16)
    )
    keep = (lax.rem(iota((80, 256), 0), 8) == lax.rem(iota((80, 256), 1), 8)) | (
        iota((80, 256), 1) == 160
    )
    lin_left[...] = jnp.where(keep, per_row, 0.0).astype(BF16)

    below_rows, above_rows = block_rows(from_below), block_rows(from_above)
    gy_all = gy[...].astype(F32)
    coarse_scale = jnp.where(is_coarse, 1.0, 0.0)
    left[:, 0:64] = gy[...]
    for part, mask in (
        (1, own_rows[:, 2:3]),
        (2, below_rows[:, 1:2]),
        (3, above_rows[:, 0:1]),
    ):
        left[:, part * 64 : part * 64 + 64] = (gy_all * (hot(mask > -0.5) * coarse_scale)).astype(BF16)
    right[...] = jnp.zeros(right.shape, BF16)
    mixed[...] = jnp.zeros(mixed.shape, BF16)

    def couple_start(first, last):
        @pl.when(is_coarse)
        def _():
            @pl.loop(first, last)
            def _(piece):
                couple(piece).start()

    z_wait()
    send_w[...] = dot(perm_b[...], recv_z[...]).astype(BF16)
    w_start()

    @pl.when(is_coarse)
    def _():
        near_wait()
        slot, cell = iota((NY, 128), 1), iota((NY, 128), 0)
        code = jnp.where(slot < 64, own_rows[:, 0:1], own_rows[:, 1:2])
        inner = lax.rem(slot, 64)
        pick = ((inner // ROWS).astype(F32) == code) & (lax.rem(inner, ROWS) == lax.rem(cell, ROWS))
        moved = dot(hot(pick).astype(BF16), near_recv[...])
        kept = hot(own_rows[:, 2:3] > -0.5)
        value = (moved + packed[...].astype(F32) * kept).astype(BF16)
        for piece in range(CH + 1):
            coupled[piece] = value[:, piece * 128 : piece * 128 + 128]


    load_w.wait()
    w_wait()

    couple_start(LATE, LATE + MIDDLE)
    spread_a = dot_tn(recv_w[...], fx[0])
    spread_b = dot_tn(recv_w[...], fx[1])
    coeffs = (spread_a[0:320] + spread_b[320:640]).astype(BF16).astype(F32)

    def mix(first, chan):
        total = jnp.zeros((32, M), F32)
        for i in range(CH):
            total = total + wts[i, first + chan].astype(F32) * coeffs[i * 32 : i * 32 + 32]
        return total

    for chan in range(CH):
        mix_send[chan] = mix((1 - ch) * CH, chan).astype(BF16)
    mix_copy = remote(mix_send, mix_recv, mix_sem.at[0], mix_sem.at[1], twin)
    mix_copy.start()
    own = [mix(ch * CH, chan) for chan in range(CH)]
    mix_copy.wait_recv()
    for chan in range(CH):
        value = (own[chan] + mix_recv[chan].astype(F32)).astype(BF16)
        mixed[0, chan * 32 : chan * 32 + 32, :] = value
        mixed[1, 320 + chan * 32 : 320 + chan * 32 + 32, :] = value
    send_v[...] = (dot_nt(gx[0], mixed[0]) + dot_nt(gx[1], mixed[1])).astype(BF16)
    v_start()
    v_wait()
    send_u[...] = dot_tn(perm_b[...], recv_v[...]).astype(BF16)
    u_start()
    couple_start(0, LATE)

    to_peer.wait_recv()
    ones_row = hot(iota((16, 256), 0) == 0).astype(BF16)

    def channel_map(first, second):
        @pl.loop(0, NY // 8)
        def _(block):
            here = pl.ds(pl.multiple_of(block * 8, 8), 8)
            planes = []
            for plane in range(PLANES):
                planes.append(
                    jnp.concatenate(
                        [first[chan, plane, here, :] for chan in range(CH)]
                        + [second[chan, plane, here, :] for chan in range(CH)],
                        axis=0,
                    )
                )
            cells = jnp.concatenate([jnp.concatenate(planes, axis=1), ones_row], axis=0)
            total = dot(lin_left[:, 0:176], cells)
            for chan in range(CH):
                base[chan, here, :] = total[chan * 8 : chan * 8 + 8]

    @pl.when(ch == 0)
    def _():
        channel_map(fld, peer)

    @pl.when(ch == 1)
    def _():
        channel_map(peer, fld)


    def interpolate(first, last):
        @pl.loop(first, last)
        def _(chan):
            couple(chan).wait_recv()
            cells = coupled_in[chan]
            row, col = iota((128, 256), 0) - 4 * chan, iota((128, 256), 1)
            pick = (
                ((row == 0) & (col == 0))
                | ((row == 1) & (col == 127))
                | ((row == 2) & (col == 128))
                | ((row == 3) & (col == 255))
            )
            value = dot(cells, unpack[...]) + dot(
                coupled_in[CH], jnp.where(pick, 0.25, 0.0).astype(BF16)
            )
            base[chan] = base[chan] + value.astype(BF16).astype(F32)

    @pl.when(pool == 1)
    def _():
        couple(CH).wait_recv()
        interpolate(LATE, CH)

    def expand(rows, table, part):
        ordered = dot_tn(perm_a[...], rows).astype(BF16)
        for group in range(5):
            spread_left = jnp.concatenate(
                [ordered[half * 64 : half * 64 + 64, group * 128 : group * 128 + 128] for half in range(2)],
                axis=1,
            )
            value = dot(spread_left, table).astype(BF16)
            for lane in range(4):
                plane, chan = (group * 4 + lane) // CH, (group * 4 + lane) % CH
                right[chan, part * 64 : part * 64 + 64, plane * 128 : plane * 128 + 128] = value[
                    :, lane * 128 : lane * 128 + 128
                ]

    def near_first(step):
        apart = ((step + 1) // 2) * (1 - 2 * lax.rem(step, 2))
        return lax.rem(zed + apart + RZ, RZ)

    def chunk(ref, index):
        return ref.at[pl.ds(pl.multiple_of(index * 8, 8), 8), :]

    def modes_out(origin):
        return remote(
            chunk(recv_u, origin), chunk(modes_in.at[0], origin), out_send.at[origin], out_recv.at[origin], other_pool
        )

    def modes_near(origin):
        source_ref = chunk(modes_in.at[0], origin)
        return neighbours(
            remote(source_ref, chunk(modes_in.at[1], origin), up_send.at[origin], up_recv.at[origin], up),
            remote(source_ref, chunk(modes_in.at[2], origin), down_send.at[origin], down_recv.at[origin], down),
        )

    @pl.loop(0, RZ)
    def _(step):
        origin = near_first(step)

        @pl.when(origin != zed)
        def _():
            u_from(origin).wait_recv()

        @pl.when(pool == 1)
        def _():
            modes_out(origin).start()

        @pl.when(is_coarse)
        def _():
            modes_out(origin).wait_recv()
            modes_near(origin)[0]()

    expand(recv_u[...], bdi[...], 0)

    @pl.when(is_coarse)
    def _():
        expand(modes_in[0], bdc[...], 1)

        @pl.loop(0, RZ)
        def _(step):
            modes_near(near_first(step))[1]()

        expand(modes_in[1], bdc[...], 2)
        expand(modes_in[2], bdc[...], 3)

    @pl.when(pool == 1)
    def _():
        interpolate(0, LATE)

    def store(chan):
        return pltpu.make_async_copy(result.at[chan], out.at[0, chan], out_sem.at[chan])

    @pl.loop(0, CH)
    def _(chan):
        total = dot(left[...], right[chan]) + base[chan]
        value = (total * (1.0 + lax.erf(total * np.float32(np.sqrt(0.5)))) * 0.5).astype(BF16)
        for plane in range(PLANES):
            result[chan, plane] = value[:, plane * 128 : plane * 128 + 128]
        store(chan).start()

    z_sent()
    w_sent()
    v_sent()
    u_sent()
    code_sent()
    to_peer.wait_send()
    mix_copy.wait_send()

    @pl.when(is_coarse)
    def _():
        near_sent()

        @pl.loop(0, CH + 1)
        def _(piece):
            couple(piece).wait_send()

        @pl.loop(0, RZ)
        def _(step):
            modes_near(near_first(step))[2]()

    @pl.when(pool == 1)
    def _():
        @pl.loop(0, RZ)
        def _(step):
            modes_out(near_first(step)).wait_send()

    @pl.loop(0, CH)
    def _(chan):
        store(chan).wait()


def body(fields, mode_weights, lin_weights, bias, source):
    weights = jnp.swapaxes(mode_weights[0], 2, 3)
    lin = jnp.swapaxes(lin_weights[0], 0, 1)
    tables = make_tables()
    anywhere = pl.BlockSpec(memory_space=pl.ANY)
    dma = pltpu.SemaphoreType.DMA
    scratch = [pltpu.VMEM(lin.shape, BF16), pltpu.VMEM(bias.shape, BF16), pltpu.VMEM(source.shape, jnp.int32)]
    scratch += [pltpu.VMEM(table.shape, BF16) for table in tables] + [
        pltpu.VMEM((CH, PLANES, NY, NZ), BF16),
        pltpu.VMEM((CH, PLANES, NY, NZ), BF16),
        pltpu.VMEM((CH, 2 * CH, 32, M), BF16),
        pltpu.VMEM((320, 512), BF16),
        pltpu.VMEM((128, LANES), BF16),
        pltpu.VMEM((128, LANES), BF16),
        pltpu.VMEM((128, LANES), BF16),
        pltpu.VMEM((128, LANES), BF16),
        pltpu.VMEM((128, LANES), BF16),
        pltpu.VMEM((CH, 32, M), BF16),
        pltpu.VMEM((CH, 32, M), BF16),
        pltpu.VMEM((2, LANES, M), BF16),
        pltpu.VMEM((128, LANES), BF16),
        pltpu.VMEM((128, LANES), BF16),
        pltpu.VMEM((128, LANES), BF16),
        pltpu.VMEM((128, LANES), BF16),
        pltpu.VMEM((8, 128), F32),
        pltpu.VMEM((2, 8, 128), F32),
        pltpu.VMEM((CH, NY, 256), F32),
        pltpu.VMEM((80, 256), BF16),
        pltpu.VMEM((NY, PACKED), BF16),
        pltpu.VMEM((128, PACKED), BF16),
        pltpu.VMEM((128, PACKED), BF16),
        pltpu.VMEM((CH + 1, NY, 128), BF16),
        pltpu.VMEM((CH + 1, NY, 128), BF16),
        pltpu.VMEM((3, 128, LANES), BF16),
        pltpu.VMEM((NY, 256), BF16),
        pltpu.VMEM((CH, 256, 256), BF16),
        pltpu.VMEM((CH, PLANES, NY, NZ), BF16),
        dma, dma,
        dma((RZ,)), dma((RZ,)), dma((RW,)), dma((RW,)), dma((RW,)), dma((RW,)), dma((RZ,)), dma((RZ,)),
        dma((2,)), dma((4,)), dma((2,)), dma((4,)), dma((CH + 1,)), dma((CH + 1,)), dma((len(NAMES) + 3,)),
        dma((RZ,)), dma((RZ,)), dma((RZ,)), dma((RZ,)), dma((RZ,)), dma((RZ,)), dma((CH,)),
    ]
    return pl.pallas_call(
        kernel,
        out_shape=jax.ShapeDtypeStruct(fields.shape, BF16),
        in_specs=[anywhere] * (5 + len(NAMES)),
        out_specs=anywhere,
        scratch_shapes=scratch,
        compiler_params=pltpu.CompilerParams(
            collective_id=0, has_side_effects=True, vmem_limit_bytes=60 * 2**20
        ),
    )(fields, weights, lin, bias, source, *tables)


def solution(mesh):
    return jax.shard_map(
        body,
        mesh=mesh,
        in_specs=(
            P("pool", "ch", "slab", None, None),
            P("pool", "ch", None, None, "slab"),
            P("pool", None, "ch"),
            P("pool", "ch"),
            P("slab", None),
        ),
        out_specs=P("pool", "ch", "slab", None, None),
        check_vma=False,
    )
```

```python
import functools

import jax
import jax.numpy as jnp
import numpy as np
from jax import lax
from jax.experimental import pallas as pl
from jax.experimental.pallas import tpu as pltpu
from jax.sharding import PartitionSpec as P

MESH = pl.DeviceIdType.MESH
BF16 = jnp.bfloat16
F32 = jnp.float32

CH, PLANES, NY, NZ, M = 10, 2, 224, 128, 64
NX = 256
RZ, RW = 16, 8
PC = CH * PLANES
LANES = PC * 32
BLOCKS, ROWS = 8, 28
PACKED = CH * 128 + 128
LATE, MIDDLE = 8, 3
NAMES = ("fy", "bdf", "perm_a", "perm_b", "pack", "gy", "fx", "gx", "bdi", "bdc", "unpack")


def dft(length):
    cells = np.arange(length, dtype=np.float32)
    order = np.arange(M, dtype=np.int32)
    half = M // 2
    freq = np.where(order < half, order, order - half + 1).astype(np.float32)
    angle = np.float32(2.0 * np.pi) * freq[:, None] * cells[None, :] / np.float32(length)
    forward = np.where((order < half)[:, None], np.cos(angle), np.sin(angle)).astype(np.float32)
    return forward, (forward.T * np.float32(2.0 / length)).astype(np.float32)


def rounded(array):
    return np.asarray(array, np.float32).astype(BF16)


def interp():
    fine = np.arange(NZ)[:, None]
    coarse = np.arange(NZ)[None, :]
    centre = NZ // 4 + fine // 2
    second = centre - 1 + 2 * (fine % 2)
    return (0.75 * (coarse == centre) + 0.25 * (coarse == second)).astype(np.float32)


def make_tables():
    fwd_x, inv_x = (rounded(table).astype(np.float32) for table in dft(NX))
    fwd_y, inv_y = (rounded(table).astype(np.float32) for table in dft(NY))
    fwd_z, inv_z = (rounded(table).astype(np.float32) for table in dft(NZ))
    mat = interp()
    inv_c = (0.5 * mat).T @ inv_z
    bdf = np.zeros((4, NZ, 2, 4, 32), np.float32)
    bdi = np.zeros((2, 4, 32, 4, NZ), np.float32)
    bdc = np.zeros((2, 4, 32, 4, NZ), np.float32)
    for group in range(4):
        for half in range(2):
            part = slice(half * 32, half * 32 + 32)
            bdf[group, :, half, group, :] = fwd_z[part].T
            bdi[half, group, :, group, :] = inv_z[:, part].T
            bdc[half, group, :, group, :] = inv_c[:, part].T
    perm_a = np.zeros((128, 128), np.float32)
    perm_b = np.zeros((128, 128), np.float32)
    for z in range(RZ):
        for w in range(RW):
            perm_a[z * 8 + w, (w % 2) * 64 + z * 4 + w // 2] = 1.0
            perm_b[w * 16 + z, z * 8 + w] = 1.0
    fx = np.zeros((2, 128, M), np.float32)
    gx = np.zeros((2, 128, M), np.float32)
    for z in range(RZ):
        for w in range(RW):
            for plane in range(2):
                cell = 2 * (z * 8 + w) + plane
                fx[plane, w * 16 + z] = fwd_x[:, cell]
                gx[plane, w * 16 + z] = inv_x[cell]
    pack = np.zeros((2, NZ, 128), np.float32)
    unpack = np.zeros((128, 2, NZ), np.float32)
    for plane in range(2):
        for cell in range(64):
            pack[plane, 32 + cell, plane * 64 + cell] = 1.0
            unpack[plane * 64 + cell, plane, :] = mat[:, 32 + cell]
    values = {
        "fy": fwd_y,
        "gy": inv_y,
        "fx": fx,
        "gx": gx,
        "bdf": bdf.reshape(512, 256),
        "bdi": bdi.reshape(256, 512),
        "bdc": bdc.reshape(256, 512),
        "perm_a": perm_a,
        "perm_b": perm_b,
        "pack": pack.reshape(256, 128),
        "unpack": unpack.reshape(128, 256),
    }
    return [rounded(values[name]) for name in NAMES]


def dot(left, right):
    return lax.dot_general(left, right, (((1,), (0,)), ((), ())), preferred_element_type=F32)


def dot_nt(left, right):
    return lax.dot_general(left, right, (((1,), (1,)), ((), ())), preferred_element_type=F32)


def dot_tn(left, right):
    return lax.dot_general(left, right, (((0,), (0,)), ((), ())), preferred_element_type=F32)


def iota(shape, axis):
    return lax.broadcasted_iota(jnp.int32, shape, axis)


def hot(mask):
    return jnp.where(mask, 1.0, 0.0)


def kernel(
    field, weights, lin_hbm, bias_hbm, source_hbm, *rest,
):
    tables, (out, lin, bias, source), rest = rest[: len(NAMES)], rest[len(NAMES) : len(NAMES) + 4], rest[len(NAMES) + 4 :]
    run(field, weights, lin_hbm, bias_hbm, source_hbm, tables, out, lin, bias, source, rest[: len(NAMES)], *rest)


def run(
    field, weights, lin_hbm, bias_hbm, source_hbm, tables_hbm, out, lin, bias, source, tables,
    fy, bdf, perm_a, perm_b, pack, gy, fx, gx, bdi, bdc, unpack,
    fld, peer, wts, along, rows_a, send_z, recv_z, send_w, recv_w, mix_send, mix_recv, mixed,
    send_v, recv_v, send_u, recv_u, codes, codes_in, base, lin_left, packed, near_send, near_recv,
    coupled, coupled_in, modes_in, left, right, result,
    load_sem, wts_sem, z_send, z_recv, w_send, w_recv, v_send, v_recv, u_send, u_recv,
    peer_sem, code_sem, mix_sem, near_sem, couple_send, couple_recv, table_sem,
    out_send, out_recv, up_send, up_recv, down_send, down_recv, out_sem,
):
    pool = lax.axis_index("pool")
    slab = lax.axis_index("slab")
    ch = lax.axis_index("ch")
    zed, wid = slab // RW, lax.rem(slab, RW)
    count = RZ * RW
    above, below = lax.rem(slab + 1, count), lax.rem(slab + count - 1, count)
    is_coarse = pool == 0
    has_up, has_down = slab < count - 1, slab > 0

    def at_z(target):
        return (pool, target * RW + wid, ch)

    def at_w(target):
        return (pool, zed * RW + target, ch)

    twin = (pool, slab, 1 - ch)
    other_pool = (1 - pool, slab, ch)
    up, down = (pool, above, ch), (pool, below, ch)

    def remote(src, dst, send, recv, device):
        return pltpu.make_async_remote_copy(
            src_ref=src, dst_ref=dst, send_sem=send, recv_sem=recv, device_id=device, device_id_type=MESH
        )

    barrier = pltpu.get_barrier_semaphore()

    def greet(device):
        pl.semaphore_signal(barrier, inc=1, device_id=device, device_id_type=MESH)

    @pl.loop(0, RZ - 1)
    def _(step):
        apart = RZ // 2 + ((step + 1) // 2) * (1 - 2 * lax.rem(step, 2))
        greet(at_z(lax.rem(zed + apart, RZ)))

    @pl.loop(1, RW)
    def _(step):
        greet(at_w(lax.rem(wid + step, RW)))

    greet(twin)
    greet(other_pool)

    @pl.when(has_up)
    def _():
        greet(up)

    @pl.when(has_down)
    def _():
        greet(down)

    load = pltpu.make_async_copy(field.at[0], fld, load_sem)
    load.start()
    loads = {
        name: pltpu.make_async_copy(src, dst, table_sem.at[index])
        for index, (name, src, dst) in enumerate(
            zip(
                NAMES + ("lin", "bias", "source"),
                tuple(tables_hbm) + (lin_hbm, bias_hbm, source_hbm),
                tuple(tables) + (lin, bias, source),
            )
        )
    }
    for name in NAMES[:3]:
        loads[name].start()
    load_w = pltpu.make_async_copy(weights, wts, wts_sem)

    @pl.when(slab == 0)
    def _():
        codes_in[0] = jnp.full((8, 128), -1.0, F32)
        near_recv[0:64] = jnp.zeros((64, PACKED), BF16)
        modes_in[1] = jnp.zeros((128, LANES), BF16)

    @pl.when(slab == count - 1)
    def _():
        codes_in[1] = jnp.full((8, 128), -1.0, F32)
        near_recv[64:128] = jnp.zeros((64, PACKED), BF16)
        modes_in[2] = jnp.zeros((128, LANES), BF16)

    loads["fy"].wait()
    load.wait()
    for name in NAMES[3:] + ("lin", "bias", "source"):
        loads[name].start()
    load_w.start()
    for pc in range(PC):
        plane, chan = pc // CH, pc % CH
        part = dot(fy[...], fld[chan, plane])
        group, lane = pc // 4, pc % 4
        along[group * 64 : group * 64 + 64, lane * 128 : lane * 128 + 128] = part.astype(BF16)
    loads["bdf"].wait()
    along_z = dot(along[...], bdf[...]).astype(BF16)
    for group in range(5):
        for half in range(2):
            rows_a[half * 64 : half * 64 + 64, group * 128 : group * 128 + 128] = along_z[
                group * 64 : group * 64 + 64, half * 128 : half * 128 + 128
            ]
    loads["perm_a"].wait()
    send_z[...] = dot(perm_a[...], rows_a[...]).astype(BF16)

    pl.semaphore_wait(barrier, RZ - 1 + RW - 1 + 2 + has_up.astype(jnp.int32) + has_down.astype(jnp.int32))

    def neighbours(upward, downward):
        def start():
            @pl.when(has_up)
            def _():
                upward.start()

            @pl.when(has_down)
            def _():
                downward.start()

        def wait_recv():
            @pl.when(has_down)
            def _():
                upward.wait_recv()

            @pl.when(has_up)
            def _():
                downward.wait_recv()

        def wait_send():
            @pl.when(has_up)
            def _():
                upward.wait_send()

            @pl.when(has_down)
            def _():
                downward.wait_send()

        return start, wait_recv, wait_send

    def exchange(size, mine, rows, device, src, dst, send, recv):
        def piece(ref, index):
            return ref.at[pl.ds(pl.multiple_of(index * rows, rows), rows), :]

        def copy(step):
            middle = (step + 1) // 2
            apart = size // 2 + middle * (1 - 2 * lax.rem(step, 2))
            target = lax.rem(mine + apart, size)
            return remote(piece(src, target), piece(dst, mine), send.at[target], recv.at[mine], device(target))

        def from_origin(origin):
            return remote(piece(src, origin), piece(dst, origin), send.at[origin], recv.at[origin], device(origin))

        def start():
            @pl.loop(0, size - 1)
            def _(step):
                copy(step).start()

            here = pl.ds(pl.multiple_of(mine * rows, rows), rows)
            dst[here, :] = src[here, :]

        def wait_recv():
            @pl.loop(0, size - 1)
            def _(step):
                from_origin(lax.rem(mine + step + 1, size)).wait_recv()

        def wait_send():
            @pl.loop(0, size - 1)
            def _(step):
                from_origin(lax.rem(mine + step + 1, size)).wait_send()

        return start, wait_recv, wait_send, from_origin

    z_start, z_wait, z_sent, _ = exchange(RZ, zed, 8, at_z, send_z, recv_z, z_send, z_recv)
    w_start, w_wait, w_sent, _ = exchange(RW, wid, 16, at_w, send_w, recv_w, w_send, w_recv)
    v_start, v_wait, v_sent, _ = exchange(RW, wid, 16, at_w, send_v, recv_v, v_send, v_recv)
    u_start, _, u_sent, u_from = exchange(RZ, zed, 8, at_z, send_u, recv_u, u_send, u_recv)

    z_start()
    to_peer = remote(fld, peer, peer_sem.at[0], peer_sem.at[1], twin)
    to_peer.start()
    for name in NAMES[3:] + ("lin", "bias", "source"):
        loads[name].wait()

    listed = source[...]
    lower = hot((listed == slab - 1) & (listed >= 0))
    upper = hot(listed == slab + 1)
    same = hot(listed == slab)
    before = hot(iota((BLOCKS, BLOCKS), 0) < iota((BLOCKS, BLOCKS), 1))
    lower_rank = dot(lower.astype(BF16), before.astype(BF16))
    upper_rank = dot(upper.astype(BF16), before.astype(BF16))
    codes[...] = jnp.full(codes.shape, -1.0, F32)
    codes[0:1, 0:BLOCKS] = jnp.where(lower > 0.5, lower_rank, -1.0)
    codes[1:2, 0:BLOCKS] = jnp.where(upper > 0.5, upper_rank, -1.0)
    codes[2:3, 0:BLOCKS] = same - 1.0

    code_start, code_wait, code_sent = neighbours(
        remote(codes, codes_in.at[0], code_sem.at[0], code_sem.at[1], up),
        remote(codes, codes_in.at[1], code_sem.at[2], code_sem.at[3], down),
    )
    code_start()

    near_start, near_wait, near_sent = neighbours(
        remote(near_send.at[0:64], near_recv.at[0:64], near_sem.at[0], near_sem.at[1], up),
        remote(near_send.at[64:128], near_recv.at[64:128], near_sem.at[2], near_sem.at[3], down),
    )

    def couple(piece):
        return remote(
            coupled.at[piece], coupled_in.at[piece], couple_send.at[piece], couple_recv.at[piece], other_pool
        )


    @pl.when(is_coarse)
    def _():
        edges = jnp.zeros((NY, 128), F32)
        for chan in range(CH):
            pair = jnp.concatenate([fld[chan, 0], fld[chan, 1]], axis=1)
            packed[:, chan * 128 : chan * 128 + 128] = dot(pair, pack[...]).astype(BF16)
            row, col = iota((256, 128), 0), iota((256, 128), 1) - 4 * chan
            pick = (
                ((row == 31) & (col == 0))
                | ((row == 96) & (col == 1))
                | ((row == 128 + 31) & (col == 2))
                | ((row == 128 + 96) & (col == 3))
            )
            edges = edges + dot(pair, hot(pick).astype(BF16))
        packed[:, CH * 128 :] = edges.astype(BF16)

    code_wait()
    from_below, from_above = codes_in[0], codes_in[1]

    def block_columns(code):
        table = hot(iota((8, NY), 1) // ROWS == iota((8, NY), 0)).astype(BF16)
        return dot(code[:, 0:BLOCKS].astype(BF16), table)

    def block_rows(code):
        table = hot(iota((NY, 8), 0) // ROWS == iota((NY, 8), 1)).astype(BF16)
        return dot_nt(table, code[:, 0:BLOCKS].astype(BF16))

    own_rows = block_rows(codes[...])

    @pl.when(is_coarse)
    def _():
        for part, row in ((0, block_columns(from_above)[0:1]), (1, block_columns(from_below)[1:2])):
            slot, cell = iota((64, NY), 0), iota((64, NY), 1)
            pick = ((slot // ROWS).astype(F32) == row) & (lax.rem(slot, ROWS) == lax.rem(cell, ROWS))
            chosen = dot(hot(pick).astype(BF16), packed[...])
            near_send[part * 64 : part * 64 + 64, :] = chosen.astype(BF16)
        near_start()

    spread = dot(
        lin[...], hot((iota((2 * CH, 256), 1) // 8) == iota((2 * CH, 256), 0)).astype(BF16)
    )
    shift = dot_tn(
        jnp.broadcast_to(bias[...], (8, CH)),
        hot((iota((8, 256), 0) == 0) & (iota((8, 256), 1) == 160)).astype(BF16),
    )
    per_row = dot(
        hot((iota((80, CH), 0) // 8) == iota((80, CH), 1)).astype(BF16), (spread + shift).astype(BF16)
    )
    keep = (lax.rem(iota((80, 256), 0), 8) == lax.rem(iota((80, 256), 1), 8)) | (
        iota((80, 256), 1) == 160
    )
    lin_left[...] = jnp.where(keep, per_row, 0.0).astype(BF16)

    below_rows, above_rows = block_rows(from_below), block_rows(from_above)
    gy_all = gy[...].astype(F32)
    coarse_scale = jnp.where(is_coarse, 1.0, 0.0)
    left[:, 0:64] = gy[...]
    for part, mask in (
        (1, own_rows[:, 2:3]),
        (2, below_rows[:, 1:2]),
        (3, above_rows[:, 0:1]),
    ):
        left[:, part * 64 : part * 64 + 64] = (gy_all * (hot(mask > -0.5) * coarse_scale)).astype(BF16)
    right[...] = jnp.zeros(right.shape, BF16)
    mixed[...] = jnp.zeros(mixed.shape, BF16)

    def couple_start(first, last):
        @pl.when(is_coarse)
        def _():
            @pl.loop(first, last)
            def _(piece):
                couple(piece).start()

    z_wait()
    send_w[...] = dot(perm_b[...], recv_z[...]).astype(BF16)
    w_start()

    @pl.when(is_coarse)
    def _():
        near_wait()
        slot, cell = iota((NY, 128), 1), iota((NY, 128), 0)
        code = jnp.where(slot < 64, own_rows[:, 0:1], own_rows[:, 1:2])
        inner = lax.rem(slot, 64)
        pick = ((inner // ROWS).astype(F32) == code) & (lax.rem(inner, ROWS) == lax.rem(cell, ROWS))
        moved = dot(hot(pick).astype(BF16), near_recv[...])
        kept = hot(own_rows[:, 2:3] > -0.5)
        value = (moved + packed[...].astype(F32) * kept).astype(BF16)
        for piece in range(CH + 1):
            coupled[piece] = value[:, piece * 128 : piece * 128 + 128]


    load_w.wait()
    w_wait()

    couple_start(LATE, LATE + MIDDLE)
    spread_a = dot_tn(recv_w[...], fx[0])
    spread_b = dot_tn(recv_w[...], fx[1])
    coeffs = (spread_a[0:320] + spread_b[320:640]).astype(BF16).astype(F32)

    def mix(first, chan):
        total = jnp.zeros((32, M), F32)
        for i in range(CH):
            total = total + wts[i, first + chan].astype(F32) * coeffs[i * 32 : i * 32 + 32]
        return total

    for chan in range(CH):
        mix_send[chan] = mix((1 - ch) * CH, chan).astype(BF16)
    mix_copy = remote(mix_send, mix_recv, mix_sem.at[0], mix_sem.at[1], twin)
    mix_copy.start()
    own = [mix(ch * CH, chan) for chan in range(CH)]
    mix_copy.wait_recv()
    for chan in range(CH):
        value = (own[chan] + mix_recv[chan].astype(F32)).astype(BF16)
        mixed[0, chan * 32 : chan * 32 + 32, :] = value
        mixed[1, 320 + chan * 32 : 320 + chan * 32 + 32, :] = value
    send_v[...] = (dot_nt(gx[0], mixed[0]) + dot_nt(gx[1], mixed[1])).astype(BF16)
    v_start()
    v_wait()
    send_u[...] = dot_tn(perm_b[...], recv_v[...]).astype(BF16)
    u_start()
    couple_start(0, LATE)

    to_peer.wait_recv()
    ones_row = hot(iota((16, 256), 0) == 0).astype(BF16)

    def channel_map(first, second):
        @pl.loop(0, NY // 8)
        def _(block):
            here = pl.ds(pl.multiple_of(block * 8, 8), 8)
            planes = []
            for plane in range(PLANES):
                planes.append(
                    jnp.concatenate(
                        [first[chan, plane, here, :] for chan in range(CH)]
                        + [second[chan, plane, here, :] for chan in range(CH)],
                        axis=0,
                    )
                )
            cells = jnp.concatenate([jnp.concatenate(planes, axis=1), ones_row], axis=0)
            total = dot(lin_left[:, 0:176], cells)
            for chan in range(CH):
                base[chan, here, :] = total[chan * 8 : chan * 8 + 8]

    @pl.when(ch == 0)
    def _():
        channel_map(fld, peer)

    @pl.when(ch == 1)
    def _():
        channel_map(peer, fld)


    def interpolate(first, last):
        @pl.loop(first, last)
        def _(chan):
            couple(chan).wait_recv()
            cells = coupled_in[chan]
            row, col = iota((128, 256), 0) - 4 * chan, iota((128, 256), 1)
            pick = (
                ((row == 0) & (col == 0))
                | ((row == 1) & (col == 127))
                | ((row == 2) & (col == 128))
                | ((row == 3) & (col == 255))
            )
            value = dot(cells, unpack[...]) + dot(
                coupled_in[CH], jnp.where(pick, 0.25, 0.0).astype(BF16)
            )
            base[chan] = base[chan] + value.astype(BF16).astype(F32)

    @pl.when(pool == 1)
    def _():
        couple(CH).wait_recv()
        interpolate(LATE, CH)

    def expand(sources, table, parts):
        lefts = []
        for rows in sources:
            ordered = dot_tn(perm_a[...], rows).astype(BF16)
            for group in range(5):
                lefts.append(
                    jnp.concatenate(
                        [ordered[half * 64 : half * 64 + 64, group * 128 : group * 128 + 128] for half in range(2)],
                        axis=1,
                    )
                )
        value = dot(jnp.concatenate(lefts, axis=0), table).astype(BF16)
        for index, part in enumerate(parts):
            for group in range(5):
                first = (index * 5 + group) * 64
                for lane in range(4):
                    plane, chan = (group * 4 + lane) // CH, (group * 4 + lane) % CH
                    right[chan, part * 64 : part * 64 + 64, plane * 128 : plane * 128 + 128] = value[
                        first : first + 64, lane * 128 : lane * 128 + 128
                    ]

    def near_first(step):
        apart = ((step + 1) // 2) * (1 - 2 * lax.rem(step, 2))
        return lax.rem(zed + apart + RZ, RZ)

    def chunk(ref, index):
        return ref.at[pl.ds(pl.multiple_of(index * 8, 8), 8), :]

    def modes_out(origin):
        return remote(
            chunk(recv_u, origin), chunk(modes_in.at[0], origin), out_send.at[origin], out_recv.at[origin], other_pool
        )

    def modes_near(origin):
        source_ref = chunk(modes_in.at[0], origin)
        return neighbours(
            remote(source_ref, chunk(modes_in.at[1], origin), up_send.at[origin], up_recv.at[origin], up),
            remote(source_ref, chunk(modes_in.at[2], origin), down_send.at[origin], down_recv.at[origin], down),
        )

    @pl.loop(0, RZ)
    def _(step):
        origin = near_first(step)

        @pl.when(origin != zed)
        def _():
            u_from(origin).wait_recv()

        @pl.when(pool == 1)
        def _():
            modes_out(origin).start()

        @pl.when(is_coarse)
        def _():
            modes_out(origin).wait_recv()
            modes_near(origin)[0]()

    expand((recv_u[...],), bdi[...], (0,))

    @pl.when(is_coarse)
    def _():
        expand((modes_in[0],), bdc[...], (1,))

        @pl.loop(0, RZ)
        def _(step):
            modes_near(near_first(step))[1]()

        expand((modes_in[1], modes_in[2]), bdc[...], (2, 3))

    @pl.when(pool == 1)
    def _():
        interpolate(0, LATE)

    def store(chan):
        return pltpu.make_async_copy(result.at[chan], out.at[0, chan], out_sem.at[chan])

    @pl.loop(0, CH, unroll=10)
    def _(chan):
        total = dot(left[...], right[chan]) + base[chan]
        value = (total * (1.0 + lax.erf(total * np.float32(np.sqrt(0.5)))) * 0.5).astype(BF16)
        for plane in range(PLANES):
            result[chan, plane] = value[:, plane * 128 : plane * 128 + 128]
        store(chan).start()

    z_sent()
    w_sent()
    v_sent()
    u_sent()
    code_sent()
    to_peer.wait_send()
    mix_copy.wait_send()

    @pl.when(is_coarse)
    def _():
        near_sent()

        @pl.loop(0, CH + 1)
        def _(piece):
            couple(piece).wait_send()

        @pl.loop(0, RZ)
        def _(step):
            modes_near(near_first(step))[2]()

    @pl.when(pool == 1)
    def _():
        @pl.loop(0, RZ)
        def _(step):
            modes_out(near_first(step)).wait_send()

    @pl.loop(0, CH)
    def _(chan):
        store(chan).wait()


def body(fields, mode_weights, lin_weights, bias, source):
    weights = jnp.swapaxes(mode_weights[0], 2, 3)
    lin = jnp.swapaxes(lin_weights[0], 0, 1)
    tables = make_tables()
    anywhere = pl.BlockSpec(memory_space=pl.ANY)
    dma = pltpu.SemaphoreType.DMA
    scratch = [pltpu.VMEM(lin.shape, BF16), pltpu.VMEM(bias.shape, BF16), pltpu.VMEM(source.shape, jnp.int32)]
    scratch += [pltpu.VMEM(table.shape, BF16) for table in tables] + [
        pltpu.VMEM((CH, PLANES, NY, NZ), BF16),
        pltpu.VMEM((CH, PLANES, NY, NZ), BF16),
        pltpu.VMEM((CH, 2 * CH, 32, M), BF16),
        pltpu.VMEM((320, 512), BF16),
        pltpu.VMEM((128, LANES), BF16),
        pltpu.VMEM((128, LANES), BF16),
        pltpu.VMEM((128, LANES), BF16),
        pltpu.VMEM((128, LANES), BF16),
        pltpu.VMEM((128, LANES), BF16),
        pltpu.VMEM((CH, 32, M), BF16),
        pltpu.VMEM((CH, 32, M), BF16),
        pltpu.VMEM((2, LANES, M), BF16),
        pltpu.VMEM((128, LANES), BF16),
        pltpu.VMEM((128, LANES), BF16),
        pltpu.VMEM((128, LANES), BF16),
        pltpu.VMEM((128, LANES), BF16),
        pltpu.VMEM((8, 128), F32),
        pltpu.VMEM((2, 8, 128), F32),
        pltpu.VMEM((CH, NY, 256), F32),
        pltpu.VMEM((80, 256), BF16),
        pltpu.VMEM((NY, PACKED), BF16),
        pltpu.VMEM((128, PACKED), BF16),
        pltpu.VMEM((128, PACKED), BF16),
        pltpu.VMEM((CH + 1, NY, 128), BF16),
        pltpu.VMEM((CH + 1, NY, 128), BF16),
        pltpu.VMEM((3, 128, LANES), BF16),
        pltpu.VMEM((NY, 256), BF16),
        pltpu.VMEM((CH, 256, 256), BF16),
        pltpu.VMEM((CH, PLANES, NY, NZ), BF16),
        dma, dma,
        dma((RZ,)), dma((RZ,)), dma((RW,)), dma((RW,)), dma((RW,)), dma((RW,)), dma((RZ,)), dma((RZ,)),
        dma((2,)), dma((4,)), dma((2,)), dma((4,)), dma((CH + 1,)), dma((CH + 1,)), dma((len(NAMES) + 3,)),
        dma((RZ,)), dma((RZ,)), dma((RZ,)), dma((RZ,)), dma((RZ,)), dma((RZ,)), dma((CH,)),
    ]
    return pl.pallas_call(
        kernel,
        out_shape=jax.ShapeDtypeStruct(fields.shape, BF16),
        in_specs=[anywhere] * (5 + len(NAMES)),
        out_specs=anywhere,
        scratch_shapes=scratch,
        compiler_params=pltpu.CompilerParams(
            collective_id=0, has_side_effects=True, vmem_limit_bytes=60 * 2**20
        ),
    )(fields, weights, lin, bias, source, *tables)


def solution(mesh):
    return jax.shard_map(
        body,
        mesh=mesh,
        in_specs=(
            P("pool", "ch", "slab", None, None),
            P("pool", "ch", None, None, "slab"),
            P("pool", None, "ch"),
            P("pool", "ch"),
            P("slab", None),
        ),
        out_specs=P("pool", "ch", "slab", None, None),
        check_vma=False,
    )
```

```python
import functools

import jax
import jax.numpy as jnp
import numpy as np
from jax import lax
from jax.experimental import pallas as pl
from jax.experimental.pallas import tpu as pltpu
from jax.sharding import PartitionSpec as P

MESH = pl.DeviceIdType.MESH
BF16 = jnp.bfloat16
F32 = jnp.float32

CH, PLANES, NY, NZ, M = 10, 2, 224, 128, 64
NX = 256
RZ, RW = 16, 8
PC = CH * PLANES
LANES = PC * 32
BLOCKS, ROWS = 8, 28
PACKED = CH * 128 + 128
LATE, MIDDLE = 6, 5
NAMES = ("fy", "bdf", "perm_a", "perm_b", "pack", "gy", "fx", "gx", "bdi", "bdc", "unpack")


def dft(length):
    cells = np.arange(length, dtype=np.float32)
    order = np.arange(M, dtype=np.int32)
    half = M // 2
    freq = np.where(order < half, order, order - half + 1).astype(np.float32)
    angle = np.float32(2.0 * np.pi) * freq[:, None] * cells[None, :] / np.float32(length)
    forward = np.where((order < half)[:, None], np.cos(angle), np.sin(angle)).astype(np.float32)
    return forward, (forward.T * np.float32(2.0 / length)).astype(np.float32)


def rounded(array):
    return np.asarray(array, np.float32).astype(BF16)


def interp():
    fine = np.arange(NZ)[:, None]
    coarse = np.arange(NZ)[None, :]
    centre = NZ // 4 + fine // 2
    second = centre - 1 + 2 * (fine % 2)
    return (0.75 * (coarse == centre) + 0.25 * (coarse == second)).astype(np.float32)


def make_tables():
    fwd_x, inv_x = (rounded(table).astype(np.float32) for table in dft(NX))
    fwd_y, inv_y = (rounded(table).astype(np.float32) for table in dft(NY))
    fwd_z, inv_z = (rounded(table).astype(np.float32) for table in dft(NZ))
    mat = interp()
    inv_c = (0.5 * mat).T @ inv_z
    bdf = np.zeros((4, NZ, 2, 4, 32), np.float32)
    bdi = np.zeros((2, 4, 32, 4, NZ), np.float32)
    bdc = np.zeros((2, 4, 32, 4, NZ), np.float32)
    for group in range(4):
        for half in range(2):
            part = slice(half * 32, half * 32 + 32)
            bdf[group, :, half, group, :] = fwd_z[part].T
            bdi[half, group, :, group, :] = inv_z[:, part].T
            bdc[half, group, :, group, :] = inv_c[:, part].T
    perm_a = np.zeros((128, 128), np.float32)
    perm_b = np.zeros((128, 128), np.float32)
    for z in range(RZ):
        for w in range(RW):
            perm_a[z * 8 + w, (w % 2) * 64 + z * 4 + w // 2] = 1.0
            perm_b[w * 16 + z, z * 8 + w] = 1.0
    fx = np.zeros((2, 128, M), np.float32)
    gx = np.zeros((2, 128, M), np.float32)
    for z in range(RZ):
        for w in range(RW):
            for plane in range(2):
                cell = 2 * (z * 8 + w) + plane
                fx[plane, w * 16 + z] = fwd_x[:, cell]
                gx[plane, w * 16 + z] = inv_x[cell]
    pack = np.zeros((2, NZ, 128), np.float32)
    unpack = np.zeros((128, 2, NZ), np.float32)
    for plane in range(2):
        for cell in range(64):
            pack[plane, 32 + cell, plane * 64 + cell] = 1.0
            unpack[plane * 64 + cell, plane, :] = mat[:, 32 + cell]
    values = {
        "fy": fwd_y,
        "gy": inv_y,
        "fx": fx,
        "gx": gx,
        "bdf": bdf.reshape(512, 256),
        "bdi": bdi.reshape(256, 512),
        "bdc": bdc.reshape(256, 512),
        "perm_a": perm_a,
        "perm_b": perm_b,
        "pack": pack.reshape(256, 128),
        "unpack": unpack.reshape(128, 256),
    }
    return [rounded(values[name]) for name in NAMES]


def dot(left, right):
    return lax.dot_general(left, right, (((1,), (0,)), ((), ())), preferred_element_type=F32)


def dot_nt(left, right):
    return lax.dot_general(left, right, (((1,), (1,)), ((), ())), preferred_element_type=F32)


def dot_tn(left, right):
    return lax.dot_general(left, right, (((0,), (0,)), ((), ())), preferred_element_type=F32)


def iota(shape, axis):
    return lax.broadcasted_iota(jnp.int32, shape, axis)


def hot(mask):
    return jnp.where(mask, 1.0, 0.0)


def kernel(
    field, weights, lin_hbm, bias_hbm, source_hbm, *rest,
):
    tables, (out, lin, bias, source), rest = rest[: len(NAMES)], rest[len(NAMES) : len(NAMES) + 4], rest[len(NAMES) + 4 :]
    run(field, weights, lin_hbm, bias_hbm, source_hbm, tables, out, lin, bias, source, rest[: len(NAMES)], *rest)


def run(
    field, weights, lin_hbm, bias_hbm, source_hbm, tables_hbm, out, lin, bias, source, tables,
    fy, bdf, perm_a, perm_b, pack, gy, fx, gx, bdi, bdc, unpack,
    fld, peer, wts, along, rows_a, send_z, recv_z, send_w, recv_w, mix_send, mix_recv, mixed,
    send_v, recv_v, send_u, recv_u, codes, codes_in, base, lin_left, packed, near_send, near_recv,
    coupled, coupled_in, modes_in, left, right, result,
    load_sem, wts_sem, z_send, z_recv, w_send, w_recv, v_send, v_recv, u_send, u_recv,
    peer_sem, code_sem, mix_sem, near_sem, couple_send, couple_recv, table_sem,
    out_send, out_recv, up_send, up_recv, down_send, down_recv, out_sem,
):
    pool = lax.axis_index("pool")
    slab = lax.axis_index("slab")
    ch = lax.axis_index("ch")
    zed, wid = slab // RW, lax.rem(slab, RW)
    count = RZ * RW
    above, below = lax.rem(slab + 1, count), lax.rem(slab + count - 1, count)
    is_coarse = pool == 0
    has_up, has_down = slab < count - 1, slab > 0

    def at_z(target):
        return (pool, target * RW + wid, ch)

    def at_w(target):
        return (pool, zed * RW + target, ch)

    twin = (pool, slab, 1 - ch)
    other_pool = (1 - pool, slab, ch)
    up, down = (pool, above, ch), (pool, below, ch)

    def remote(src, dst, send, recv, device):
        return pltpu.make_async_remote_copy(
            src_ref=src, dst_ref=dst, send_sem=send, recv_sem=recv, device_id=device, device_id_type=MESH
        )

    barrier = pltpu.get_barrier_semaphore()

    def greet(device):
        pl.semaphore_signal(barrier, inc=1, device_id=device, device_id_type=MESH)

    @pl.loop(0, RZ - 1)
    def _(step):
        apart = RZ // 2 + ((step + 1) // 2) * (1 - 2 * lax.rem(step, 2))
        greet(at_z(lax.rem(zed + apart, RZ)))

    @pl.loop(1, RW)
    def _(step):
        greet(at_w(lax.rem(wid + step, RW)))

    greet(twin)
    greet(other_pool)

    @pl.when(has_up)
    def _():
        greet(up)

    @pl.when(has_down)
    def _():
        greet(down)

    load = pltpu.make_async_copy(field.at[0], fld, load_sem)
    load.start()
    loads = {
        name: pltpu.make_async_copy(src, dst, table_sem.at[index])
        for index, (name, src, dst) in enumerate(
            zip(
                NAMES + ("lin", "bias", "source"),
                tuple(tables_hbm) + (lin_hbm, bias_hbm, source_hbm),
                tuple(tables) + (lin, bias, source),
            )
        )
    }
    for name in NAMES[:3]:
        loads[name].start()
    load_w = pltpu.make_async_copy(weights, wts, wts_sem)

    @pl.when(slab == 0)
    def _():
        codes_in[0] = jnp.full((8, 128), -1.0, F32)
        near_recv[0:64] = jnp.zeros((64, PACKED), BF16)
        modes_in[1] = jnp.zeros((128, LANES), BF16)

    @pl.when(slab == count - 1)
    def _():
        codes_in[1] = jnp.full((8, 128), -1.0, F32)
        near_recv[64:128] = jnp.zeros((64, PACKED), BF16)
        modes_in[2] = jnp.zeros((128, LANES), BF16)

    loads["fy"].wait()
    load.wait()
    for name in NAMES[3:] + ("lin", "bias", "source"):
        loads[name].start()
    load_w.start()
    for pc in range(PC):
        plane, chan = pc // CH, pc % CH
        part = dot(fy[...], fld[chan, plane])
        group, lane = pc // 4, pc % 4
        along[group * 64 : group * 64 + 64, lane * 128 : lane * 128 + 128] = part.astype(BF16)
    loads["bdf"].wait()
    along_z = dot(along[...], bdf[...]).astype(BF16)
    for group in range(5):
        for half in range(2):
            rows_a[half * 64 : half * 64 + 64, group * 128 : group * 128 + 128] = along_z[
                group * 64 : group * 64 + 64, half * 128 : half * 128 + 128
            ]
    loads["perm_a"].wait()
    send_z[...] = dot(perm_a[...], rows_a[...]).astype(BF16)

    pl.semaphore_wait(barrier, RZ - 1 + RW - 1 + 2 + has_up.astype(jnp.int32) + has_down.astype(jnp.int32))

    def neighbours(upward, downward):
        def start():
            @pl.when(has_up)
            def _():
                upward.start()

            @pl.when(has_down)
            def _():
                downward.start()

        def wait_recv():
            @pl.when(has_down)
            def _():
                upward.wait_recv()

            @pl.when(has_up)
            def _():
                downward.wait_recv()

        def wait_send():
            @pl.when(has_up)
            def _():
                upward.wait_send()

            @pl.when(has_down)
            def _():
                downward.wait_send()

        return start, wait_recv, wait_send

    def exchange(size, mine, rows, device, src, dst, send, recv):
        def piece(ref, index):
            return ref.at[pl.ds(pl.multiple_of(index * rows, rows), rows), :]

        def copy(step):
            middle = (step + 1) // 2
            apart = size // 2 + middle * (1 - 2 * lax.rem(step, 2))
            target = lax.rem(mine + apart, size)
            return remote(piece(src, target), piece(dst, mine), send.at[target], recv.at[mine], device(target))

        def from_origin(origin):
            return remote(piece(src, origin), piece(dst, origin), send.at[origin], recv.at[origin], device(origin))

        def start():
            @pl.loop(0, size - 1)
            def _(step):
                copy(step).start()

            here = pl.ds(pl.multiple_of(mine * rows, rows), rows)
            dst[here, :] = src[here, :]

        def wait_recv():
            @pl.loop(0, size - 1)
            def _(step):
                from_origin(lax.rem(mine + step + 1, size)).wait_recv()

        def wait_send():
            @pl.loop(0, size - 1)
            def _(step):
                from_origin(lax.rem(mine + step + 1, size)).wait_send()

        return start, wait_recv, wait_send, from_origin

    z_start, z_wait, z_sent, _ = exchange(RZ, zed, 8, at_z, send_z, recv_z, z_send, z_recv)
    w_start, w_wait, w_sent, _ = exchange(RW, wid, 16, at_w, send_w, recv_w, w_send, w_recv)
    v_start, v_wait, v_sent, _ = exchange(RW, wid, 16, at_w, send_v, recv_v, v_send, v_recv)
    u_start, _, u_sent, u_from = exchange(RZ, zed, 8, at_z, send_u, recv_u, u_send, u_recv)

    z_start()
    to_peer = remote(fld, peer, peer_sem.at[0], peer_sem.at[1], twin)
    to_peer.start()
    for name in NAMES[3:] + ("lin", "bias", "source"):
        loads[name].wait()

    listed = source[...]
    lower = hot((listed == slab - 1) & (listed >= 0))
    upper = hot(listed == slab + 1)
    same = hot(listed == slab)
    before = hot(iota((BLOCKS, BLOCKS), 0) < iota((BLOCKS, BLOCKS), 1))
    lower_rank = dot(lower.astype(BF16), before.astype(BF16))
    upper_rank = dot(upper.astype(BF16), before.astype(BF16))
    codes[...] = jnp.full(codes.shape, -1.0, F32)
    codes[0:1, 0:BLOCKS] = jnp.where(lower > 0.5, lower_rank, -1.0)
    codes[1:2, 0:BLOCKS] = jnp.where(upper > 0.5, upper_rank, -1.0)
    codes[2:3, 0:BLOCKS] = same - 1.0

    code_start, code_wait, code_sent = neighbours(
        remote(codes, codes_in.at[0], code_sem.at[0], code_sem.at[1], up),
        remote(codes, codes_in.at[1], code_sem.at[2], code_sem.at[3], down),
    )
    code_start()

    near_start, near_wait, near_sent = neighbours(
        remote(near_send.at[0:64], near_recv.at[0:64], near_sem.at[0], near_sem.at[1], up),
        remote(near_send.at[64:128], near_recv.at[64:128], near_sem.at[2], near_sem.at[3], down),
    )

    def couple(piece):
        return remote(
            coupled.at[piece], coupled_in.at[piece], couple_send.at[piece], couple_recv.at[piece], other_pool
        )


    @pl.when(is_coarse)
    def _():
        edges = jnp.zeros((NY, 128), F32)
        for chan in range(CH):
            pair = jnp.concatenate([fld[chan, 0], fld[chan, 1]], axis=1)
            packed[:, chan * 128 : chan * 128 + 128] = dot(pair, pack[...]).astype(BF16)
            row, col = iota((256, 128), 0), iota((256, 128), 1) - 4 * chan
            pick = (
                ((row == 31) & (col == 0))
                | ((row == 96) & (col == 1))
                | ((row == 128 + 31) & (col == 2))
                | ((row == 128 + 96) & (col == 3))
            )
            edges = edges + dot(pair, hot(pick).astype(BF16))
        packed[:, CH * 128 :] = edges.astype(BF16)

    code_wait()
    from_below, from_above = codes_in[0], codes_in[1]

    def block_columns(code):
        table = hot(iota((8, NY), 1) // ROWS == iota((8, NY), 0)).astype(BF16)
        return dot(code[:, 0:BLOCKS].astype(BF16), table)

    def block_rows(code):
        table = hot(iota((NY, 8), 0) // ROWS == iota((NY, 8), 1)).astype(BF16)
        return dot_nt(table, code[:, 0:BLOCKS].astype(BF16))

    own_rows = block_rows(codes[...])

    @pl.when(is_coarse)
    def _():
        for part, row in ((0, block_columns(from_above)[0:1]), (1, block_columns(from_below)[1:2])):
            slot, cell = iota((64, NY), 0), iota((64, NY), 1)
            pick = ((slot // ROWS).astype(F32) == row) & (lax.rem(slot, ROWS) == lax.rem(cell, ROWS))
            chosen = dot(hot(pick).astype(BF16), packed[...])
            near_send[part * 64 : part * 64 + 64, :] = chosen.astype(BF16)
        near_start()

    spread = dot(
        lin[...], hot((iota((2 * CH, 256), 1) // 8) == iota((2 * CH, 256), 0)).astype(BF16)
    )
    shift = dot_tn(
        jnp.broadcast_to(bias[...], (8, CH)),
        hot((iota((8, 256), 0) == 0) & (iota((8, 256), 1) == 160)).astype(BF16),
    )
    per_row = dot(
        hot((iota((80, CH), 0) // 8) == iota((80, CH), 1)).astype(BF16), (spread + shift).astype(BF16)
    )
    keep = (lax.rem(iota((80, 256), 0), 8) == lax.rem(iota((80, 256), 1), 8)) | (
        iota((80, 256), 1) == 160
    )
    lin_left[...] = jnp.where(keep, per_row, 0.0).astype(BF16)

    below_rows, above_rows = block_rows(from_below), block_rows(from_above)
    gy_all = gy[...].astype(F32)
    coarse_scale = jnp.where(is_coarse, 1.0, 0.0)
    left[:, 0:64] = gy[...]
    for part, mask in (
        (1, own_rows[:, 2:3]),
        (2, below_rows[:, 1:2]),
        (3, above_rows[:, 0:1]),
    ):
        left[:, part * 64 : part * 64 + 64] = (gy_all * (hot(mask > -0.5) * coarse_scale)).astype(BF16)
    right[...] = jnp.zeros(right.shape, BF16)
    mixed[...] = jnp.zeros(mixed.shape, BF16)

    z_wait()
    send_w[...] = dot(perm_b[...], recv_z[...]).astype(BF16)
    w_start()

    @pl.when(is_coarse)
    def _():
        near_wait()
        slot, cell = iota((NY, 128), 1), iota((NY, 128), 0)
        code = jnp.where(slot < 64, own_rows[:, 0:1], own_rows[:, 1:2])
        inner = lax.rem(slot, 64)
        pick = ((inner // ROWS).astype(F32) == code) & (lax.rem(inner, ROWS) == lax.rem(cell, ROWS))
        moved = dot(hot(pick).astype(BF16), near_recv[...])
        kept = hot(own_rows[:, 2:3] > -0.5)
        value = (moved + packed[...].astype(F32) * kept).astype(BF16)
        for piece in range(CH + 1):
            coupled[piece] = value[:, piece * 128 : piece * 128 + 128]

    def couple_start(first, last):
        @pl.when(is_coarse)
        def _():
            @pl.loop(first, last)
            def _(piece):
                couple(piece).start()

    couple_start(LATE, LATE + MIDDLE)


    load_w.wait()
    w_wait()

    spread_a = dot_tn(recv_w[...], fx[0])
    spread_b = dot_tn(recv_w[...], fx[1])
    coeffs = (spread_a[0:320] + spread_b[320:640]).astype(BF16).astype(F32)

    def mix(first, chan):
        total = jnp.zeros((32, M), F32)
        for i in range(CH):
            total = total + wts[i, first + chan].astype(F32) * coeffs[i * 32 : i * 32 + 32]
        return total

    for chan in range(CH):
        mix_send[chan] = mix((1 - ch) * CH, chan).astype(BF16)
    mix_copy = remote(mix_send, mix_recv, mix_sem.at[0], mix_sem.at[1], twin)
    mix_copy.start()
    own = [mix(ch * CH, chan) for chan in range(CH)]
    mix_copy.wait_recv()
    for chan in range(CH):
        value = (own[chan] + mix_recv[chan].astype(F32)).astype(BF16)
        mixed[0, chan * 32 : chan * 32 + 32, :] = value
        mixed[1, 320 + chan * 32 : 320 + chan * 32 + 32, :] = value
    send_v[...] = (dot_nt(gx[0], mixed[0]) + dot_nt(gx[1], mixed[1])).astype(BF16)
    v_start()
    v_wait()
    send_u[...] = dot_tn(perm_b[...], recv_v[...]).astype(BF16)
    u_start()
    couple_start(0, LATE)

    to_peer.wait_recv()
    ones_row = hot(iota((16, 256), 0) == 0).astype(BF16)

    def channel_map(first, second):
        @pl.loop(0, NY // 8)
        def _(block):
            here = pl.ds(pl.multiple_of(block * 8, 8), 8)
            planes = []
            for plane in range(PLANES):
                planes.append(
                    jnp.concatenate(
                        [first[chan, plane, here, :] for chan in range(CH)]
                        + [second[chan, plane, here, :] for chan in range(CH)],
                        axis=0,
                    )
                )
            cells = jnp.concatenate([jnp.concatenate(planes, axis=1), ones_row], axis=0)
            total = dot(lin_left[:, 0:176], cells)
            for chan in range(CH):
                base[chan, here, :] = total[chan * 8 : chan * 8 + 8]

    @pl.when(ch == 0)
    def _():
        channel_map(fld, peer)

    @pl.when(ch == 1)
    def _():
        channel_map(peer, fld)


    def interpolate(first, last):
        @pl.loop(first, last)
        def _(chan):
            couple(chan).wait_recv()
            cells = coupled_in[chan]
            row, col = iota((128, 256), 0) - 4 * chan, iota((128, 256), 1)
            pick = (
                ((row == 0) & (col == 0))
                | ((row == 1) & (col == 127))
                | ((row == 2) & (col == 128))
                | ((row == 3) & (col == 255))
            )
            value = dot(cells, unpack[...]) + dot(
                coupled_in[CH], jnp.where(pick, 0.25, 0.0).astype(BF16)
            )
            base[chan] = base[chan] + value.astype(BF16).astype(F32)

    @pl.when(pool == 1)
    def _():
        couple(CH).wait_recv()
        interpolate(LATE, CH)

    def expand(sources, table, parts):
        lefts = []
        for rows in sources:
            ordered = dot_tn(perm_a[...], rows).astype(BF16)
            for group in range(5):
                lefts.append(
                    jnp.concatenate(
                        [ordered[half * 64 : half * 64 + 64, group * 128 : group * 128 + 128] for half in range(2)],
                        axis=1,
                    )
                )
        value = dot(jnp.concatenate(lefts, axis=0), table).astype(BF16)
        for index, part in enumerate(parts):
            for group in range(5):
                first = (index * 5 + group) * 64
                for lane in range(4):
                    plane, chan = (group * 4 + lane) // CH, (group * 4 + lane) % CH
                    right[chan, part * 64 : part * 64 + 64, plane * 128 : plane * 128 + 128] = value[
                        first : first + 64, lane * 128 : lane * 128 + 128
                    ]

    def near_first(step):
        apart = ((step + 1) // 2) * (1 - 2 * lax.rem(step, 2))
        return lax.rem(zed + apart + RZ, RZ)

    def chunk(ref, index):
        return ref.at[pl.ds(pl.multiple_of(index * 8, 8), 8), :]

    def modes_out(origin):
        return remote(
            chunk(recv_u, origin), chunk(modes_in.at[0], origin), out_send.at[origin], out_recv.at[origin], other_pool
        )

    def modes_near(origin):
        source_ref = chunk(modes_in.at[0], origin)
        return neighbours(
            remote(source_ref, chunk(modes_in.at[1], origin), up_send.at[origin], up_recv.at[origin], up),
            remote(source_ref, chunk(modes_in.at[2], origin), down_send.at[origin], down_recv.at[origin], down),
        )

    @pl.loop(0, RZ)
    def _(step):
        origin = near_first(step)

        @pl.when(origin != zed)
        def _():
            u_from(origin).wait_recv()

        @pl.when(pool == 1)
        def _():
            modes_out(origin).start()

        @pl.when(is_coarse)
        def _():
            modes_out(origin).wait_recv()
            modes_near(origin)[0]()

    expand((recv_u[...],), bdi[...], (0,))

    @pl.when(is_coarse)
    def _():
        expand((modes_in[0],), bdc[...], (1,))

        @pl.loop(0, RZ)
        def _(step):
            modes_near(near_first(step))[1]()

        expand((modes_in[1], modes_in[2]), bdc[...], (2, 3))

    @pl.when(pool == 1)
    def _():
        interpolate(0, LATE)

    def store(chan):
        return pltpu.make_async_copy(result.at[chan], out.at[0, chan], out_sem.at[chan])

    @pl.loop(0, CH, unroll=5)
    def _(chan):
        total = dot(left[...], right[chan]) + base[chan]
        value = (total * (1.0 + lax.erf(total * np.float32(np.sqrt(0.5)))) * 0.5).astype(BF16)
        for plane in range(PLANES):
            result[chan, plane] = value[:, plane * 128 : plane * 128 + 128]
        store(chan).start()

    z_sent()
    w_sent()
    v_sent()
    u_sent()
    code_sent()
    to_peer.wait_send()
    mix_copy.wait_send()

    @pl.when(is_coarse)
    def _():
        near_sent()

        @pl.loop(0, CH + 1)
        def _(piece):
            couple(piece).wait_send()

        @pl.loop(0, RZ)
        def _(step):
            modes_near(near_first(step))[2]()

    @pl.when(pool == 1)
    def _():
        @pl.loop(0, RZ)
        def _(step):
            modes_out(near_first(step)).wait_send()

    @pl.loop(0, CH)
    def _(chan):
        store(chan).wait()


def body(fields, mode_weights, lin_weights, bias, source):
    weights = jnp.swapaxes(mode_weights[0], 2, 3)
    lin = jnp.swapaxes(lin_weights[0], 0, 1)
    tables = make_tables()
    anywhere = pl.BlockSpec(memory_space=pl.ANY)
    dma = pltpu.SemaphoreType.DMA
    scratch = [pltpu.VMEM(lin.shape, BF16), pltpu.VMEM(bias.shape, BF16), pltpu.VMEM(source.shape, jnp.int32)]
    scratch += [pltpu.VMEM(table.shape, BF16) for table in tables] + [
        pltpu.VMEM((CH, PLANES, NY, NZ), BF16),
        pltpu.VMEM((CH, PLANES, NY, NZ), BF16),
        pltpu.VMEM((CH, 2 * CH, 32, M), BF16),
        pltpu.VMEM((320, 512), BF16),
        pltpu.VMEM((128, LANES), BF16),
        pltpu.VMEM((128, LANES), BF16),
        pltpu.VMEM((128, LANES), BF16),
        pltpu.VMEM((128, LANES), BF16),
        pltpu.VMEM((128, LANES), BF16),
        pltpu.VMEM((CH, 32, M), BF16),
        pltpu.VMEM((CH, 32, M), BF16),
        pltpu.VMEM((2, LANES, M), BF16),
        pltpu.VMEM((128, LANES), BF16),
        pltpu.VMEM((128, LANES), BF16),
        pltpu.VMEM((128, LANES), BF16),
        pltpu.VMEM((128, LANES), BF16),
        pltpu.VMEM((8, 128), F32),
        pltpu.VMEM((2, 8, 128), F32),
        pltpu.VMEM((CH, NY, 256), F32),
        pltpu.VMEM((80, 256), BF16),
        pltpu.VMEM((NY, PACKED), BF16),
        pltpu.VMEM((128, PACKED), BF16),
        pltpu.VMEM((128, PACKED), BF16),
        pltpu.VMEM((CH + 1, NY, 128), BF16),
        pltpu.VMEM((CH + 1, NY, 128), BF16),
        pltpu.VMEM((3, 128, LANES), BF16),
        pltpu.VMEM((NY, 256), BF16),
        pltpu.VMEM((CH, 256, 256), BF16),
        pltpu.VMEM((CH, PLANES, NY, NZ), BF16),
        dma, dma,
        dma((RZ,)), dma((RZ,)), dma((RW,)), dma((RW,)), dma((RW,)), dma((RW,)), dma((RZ,)), dma((RZ,)),
        dma((2,)), dma((4,)), dma((2,)), dma((4,)), dma((CH + 1,)), dma((CH + 1,)), dma((len(NAMES) + 3,)),
        dma((RZ,)), dma((RZ,)), dma((RZ,)), dma((RZ,)), dma((RZ,)), dma((RZ,)), dma((CH,)),
    ]
    return pl.pallas_call(
        kernel,
        out_shape=jax.ShapeDtypeStruct(fields.shape, BF16),
        in_specs=[anywhere] * (5 + len(NAMES)),
        out_specs=anywhere,
        scratch_shapes=scratch,
        compiler_params=pltpu.CompilerParams(
            collective_id=0, has_side_effects=True, vmem_limit_bytes=60 * 2**20
        ),
    )(fields, weights, lin, bias, source, *tables)


def solution(mesh):
    return jax.shard_map(
        body,
        mesh=mesh,
        in_specs=(
            P("pool", "ch", "slab", None, None),
            P("pool", "ch", None, None, "slab"),
            P("pool", None, "ch"),
            P("pool", "ch"),
            P("slab", None),
        ),
        out_specs=P("pool", "ch", "slab", None, None),
        check_vma=False,
    )
```

```python
import functools

import jax
import jax.numpy as jnp
import numpy as np
from jax import lax
from jax.experimental import pallas as pl
from jax.experimental.pallas import tpu as pltpu
from jax.sharding import PartitionSpec as P

MESH = pl.DeviceIdType.MESH
BF16 = jnp.bfloat16
F32 = jnp.float32

CH, PLANES, NY, NZ, M = 10, 2, 224, 128, 64
NX = 256
RZ, RW = 16, 8
PC = CH * PLANES
LANES = PC * 32
BLOCKS, ROWS = 8, 28
PACKED = CH * 128 + 128
LATE, MIDDLE = 5, 6
NAMES = ("fy", "bdf", "perm_a", "perm_b", "pack", "gy", "fx", "gx", "bdi", "bdc", "unpack")


def dft(length):
    cells = np.arange(length, dtype=np.float32)
    order = np.arange(M, dtype=np.int32)
    half = M // 2
    freq = np.where(order < half, order, order - half + 1).astype(np.float32)
    angle = np.float32(2.0 * np.pi) * freq[:, None] * cells[None, :] / np.float32(length)
    forward = np.where((order < half)[:, None], np.cos(angle), np.sin(angle)).astype(np.float32)
    return forward, (forward.T * np.float32(2.0 / length)).astype(np.float32)


def rounded(array):
    return np.asarray(array, np.float32).astype(BF16)


def interp():
    fine = np.arange(NZ)[:, None]
    coarse = np.arange(NZ)[None, :]
    centre = NZ // 4 + fine // 2
    second = centre - 1 + 2 * (fine % 2)
    return (0.75 * (coarse == centre) + 0.25 * (coarse == second)).astype(np.float32)


def make_tables():
    fwd_x, inv_x = (rounded(table).astype(np.float32) for table in dft(NX))
    fwd_y, inv_y = (rounded(table).astype(np.float32) for table in dft(NY))
    fwd_z, inv_z = (rounded(table).astype(np.float32) for table in dft(NZ))
    mat = interp()
    inv_c = (0.5 * mat).T @ inv_z
    bdf = np.zeros((4, NZ, 2, 4, 32), np.float32)
    bdi = np.zeros((2, 4, 32, 4, NZ), np.float32)
    bdc = np.zeros((2, 4, 32, 4, NZ), np.float32)
    for group in range(4):
        for half in range(2):
            part = slice(half * 32, half * 32 + 32)
            bdf[group, :, half, group, :] = fwd_z[part].T
            bdi[half, group, :, group, :] = inv_z[:, part].T
            bdc[half, group, :, group, :] = inv_c[:, part].T
    perm_a = np.zeros((128, 128), np.float32)
    perm_b = np.zeros((128, 128), np.float32)
    for z in range(RZ):
        for w in range(RW):
            perm_a[z * 8 + w, (w % 2) * 64 + z * 4 + w // 2] = 1.0
            perm_b[w * 16 + z, z * 8 + w] = 1.0
    fx = np.zeros((2, 128, M), np.float32)
    gx = np.zeros((2, 128, M), np.float32)
    for z in range(RZ):
        for w in range(RW):
            for plane in range(2):
                cell = 2 * (z * 8 + w) + plane
                fx[plane, w * 16 + z] = fwd_x[:, cell]
                gx[plane, w * 16 + z] = inv_x[cell]
    pack = np.zeros((2, NZ, 128), np.float32)
    unpack = np.zeros((128, 2, NZ), np.float32)
    for plane in range(2):
        for cell in range(64):
            pack[plane, 32 + cell, plane * 64 + cell] = 1.0
            unpack[plane * 64 + cell, plane, :] = mat[:, 32 + cell]
    values = {
        "fy": fwd_y,
        "gy": inv_y,
        "fx": fx,
        "gx": gx,
        "bdf": bdf.reshape(512, 256),
        "bdi": bdi.reshape(256, 512),
        "bdc": bdc.reshape(256, 512),
        "perm_a": perm_a,
        "perm_b": perm_b,
        "pack": pack.reshape(256, 128),
        "unpack": unpack.reshape(128, 256),
    }
    return [rounded(values[name]) for name in NAMES]


def dot(left, right):
    return lax.dot_general(left, right, (((1,), (0,)), ((), ())), preferred_element_type=F32)


def dot_nt(left, right):
    return lax.dot_general(left, right, (((1,), (1,)), ((), ())), preferred_element_type=F32)


def dot_tn(left, right):
    return lax.dot_general(left, right, (((0,), (0,)), ((), ())), preferred_element_type=F32)


def iota(shape, axis):
    return lax.broadcasted_iota(jnp.int32, shape, axis)


def hot(mask):
    return jnp.where(mask, 1.0, 0.0)


def kernel(
    field, weights, lin_hbm, bias_hbm, source_hbm, *rest,
):
    tables, (out, lin, bias, source), rest = rest[: len(NAMES)], rest[len(NAMES) : len(NAMES) + 4], rest[len(NAMES) + 4 :]
    run(field, weights, lin_hbm, bias_hbm, source_hbm, tables, out, lin, bias, source, rest[: len(NAMES)], *rest)


def run(
    field, weights, lin_hbm, bias_hbm, source_hbm, tables_hbm, out, lin, bias, source, tables,
    fy, bdf, perm_a, perm_b, pack, gy, fx, gx, bdi, bdc, unpack,
    fld, peer, wts, along, rows_a, send_z, recv_z, send_w, recv_w, mix_send, mix_recv, mixed,
    send_v, recv_v, send_u, recv_u, codes, codes_in, base, lin_left, packed, near_send, near_recv,
    coupled, coupled_in, modes_in, left, right, result,
    load_sem, wts_sem, z_send, z_recv, w_send, w_recv, v_send, v_recv, u_send, u_recv,
    peer_sem, code_sem, mix_sem, near_sem, couple_send, couple_recv, table_sem,
    out_send, out_recv, up_send, up_recv, down_send, down_recv, out_sem,
):
    pool = lax.axis_index("pool")
    slab = lax.axis_index("slab")
    ch = lax.axis_index("ch")
    zed, wid = slab // RW, lax.rem(slab, RW)
    count = RZ * RW
    above, below = lax.rem(slab + 1, count), lax.rem(slab + count - 1, count)
    is_coarse = pool == 0
    has_up, has_down = slab < count - 1, slab > 0

    def at_z(target):
        return (pool, target * RW + wid, ch)

    def at_w(target):
        return (pool, zed * RW + target, ch)

    twin = (pool, slab, 1 - ch)
    other_pool = (1 - pool, slab, ch)
    up, down = (pool, above, ch), (pool, below, ch)

    def remote(src, dst, send, recv, device):
        return pltpu.make_async_remote_copy(
            src_ref=src, dst_ref=dst, send_sem=send, recv_sem=recv, device_id=device, device_id_type=MESH
        )

    barrier = pltpu.get_barrier_semaphore()

    def greet(device):
        pl.semaphore_signal(barrier, inc=1, device_id=device, device_id_type=MESH)

    @pl.loop(0, RZ - 1)
    def _(step):
        apart = RZ // 2 + ((step + 1) // 2) * (1 - 2 * lax.rem(step, 2))
        greet(at_z(lax.rem(zed + apart, RZ)))

    @pl.loop(1, RW)
    def _(step):
        greet(at_w(lax.rem(wid + step, RW)))

    greet(twin)
    greet(other_pool)

    @pl.when(has_up)
    def _():
        greet(up)

    @pl.when(has_down)
    def _():
        greet(down)

    load = pltpu.make_async_copy(field.at[0], fld, load_sem)
    load.start()
    loads = {
        name: pltpu.make_async_copy(src, dst, table_sem.at[index])
        for index, (name, src, dst) in enumerate(
            zip(
                NAMES + ("lin", "bias", "source"),
                tuple(tables_hbm) + (lin_hbm, bias_hbm, source_hbm),
                tuple(tables) + (lin, bias, source),
            )
        )
    }
    for name in NAMES[:3]:
        loads[name].start()
    load_w = pltpu.make_async_copy(weights, wts, wts_sem)

    @pl.when(slab == 0)
    def _():
        codes_in[0] = jnp.full((8, 128), -1.0, F32)
        near_recv[0:64] = jnp.zeros((64, PACKED), BF16)
        modes_in[1] = jnp.zeros((128, LANES), BF16)

    @pl.when(slab == count - 1)
    def _():
        codes_in[1] = jnp.full((8, 128), -1.0, F32)
        near_recv[64:128] = jnp.zeros((64, PACKED), BF16)
        modes_in[2] = jnp.zeros((128, LANES), BF16)

    loads["fy"].wait()
    load.wait()
    for name in NAMES[3:] + ("lin", "bias", "source"):
        loads[name].start()
    load_w.start()
    for pc in range(PC):
        plane, chan = pc // CH, pc % CH
        part = dot(fy[...], fld[chan, plane])
        group, lane = pc // 4, pc % 4
        along[group * 64 : group * 64 + 64, lane * 128 : lane * 128 + 128] = part.astype(BF16)
    loads["bdf"].wait()
    along_z = dot(along[...], bdf[...]).astype(BF16)
    for group in range(5):
        for half in range(2):
            rows_a[half * 64 : half * 64 + 64, group * 128 : group * 128 + 128] = along_z[
                group * 64 : group * 64 + 64, half * 128 : half * 128 + 128
            ]
    loads["perm_a"].wait()
    send_z[...] = dot(perm_a[...], rows_a[...]).astype(BF16)

    pl.semaphore_wait(barrier, RZ - 1 + RW - 1 + 2 + has_up.astype(jnp.int32) + has_down.astype(jnp.int32))

    def neighbours(upward, downward):
        def start():
            @pl.when(has_up)
            def _():
                upward.start()

            @pl.when(has_down)
            def _():
                downward.start()

        def wait_recv():
            @pl.when(has_down)
            def _():
                upward.wait_recv()

            @pl.when(has_up)
            def _():
                downward.wait_recv()

        def wait_send():
            @pl.when(has_up)
            def _():
                upward.wait_send()

            @pl.when(has_down)
            def _():
                downward.wait_send()

        return start, wait_recv, wait_send

    def exchange(size, mine, rows, device, src, dst, send, recv):
        def piece(ref, index):
            return ref.at[pl.ds(pl.multiple_of(index * rows, rows), rows), :]

        def copy(step):
            middle = (step + 1) // 2
            apart = size // 2 + middle * (1 - 2 * lax.rem(step, 2))
            target = lax.rem(mine + apart, size)
            return remote(piece(src, target), piece(dst, mine), send.at[target], recv.at[mine], device(target))

        def from_origin(origin):
            return remote(piece(src, origin), piece(dst, origin), send.at[origin], recv.at[origin], device(origin))

        def start():
            @pl.loop(0, size - 1)
            def _(step):
                copy(step).start()

            here = pl.ds(pl.multiple_of(mine * rows, rows), rows)
            dst[here, :] = src[here, :]

        def wait_recv():
            @pl.loop(0, size - 1)
            def _(step):
                from_origin(lax.rem(mine + step + 1, size)).wait_recv()

        def wait_send():
            @pl.loop(0, size - 1)
            def _(step):
                from_origin(lax.rem(mine + step + 1, size)).wait_send()

        return start, wait_recv, wait_send, from_origin

    z_start, z_wait, z_sent, _ = exchange(RZ, zed, 8, at_z, send_z, recv_z, z_send, z_recv)
    w_start, w_wait, w_sent, _ = exchange(RW, wid, 16, at_w, send_w, recv_w, w_send, w_recv)
    v_start, v_wait, v_sent, _ = exchange(RW, wid, 16, at_w, send_v, recv_v, v_send, v_recv)
    u_start, _, u_sent, u_from = exchange(RZ, zed, 8, at_z, send_u, recv_u, u_send, u_recv)

    z_start()
    to_peer = remote(fld, peer, peer_sem.at[0], peer_sem.at[1], twin)
    to_peer.start()
    for name in NAMES[3:] + ("lin", "bias", "source"):
        loads[name].wait()

    listed = source[...]
    lower = hot((listed == slab - 1) & (listed >= 0))
    upper = hot(listed == slab + 1)
    same = hot(listed == slab)
    before = hot(iota((BLOCKS, BLOCKS), 0) < iota((BLOCKS, BLOCKS), 1))
    lower_rank = dot(lower.astype(BF16), before.astype(BF16))
    upper_rank = dot(upper.astype(BF16), before.astype(BF16))
    codes[...] = jnp.full(codes.shape, -1.0, F32)
    codes[0:1, 0:BLOCKS] = jnp.where(lower > 0.5, lower_rank, -1.0)
    codes[1:2, 0:BLOCKS] = jnp.where(upper > 0.5, upper_rank, -1.0)
    codes[2:3, 0:BLOCKS] = same - 1.0

    code_start, code_wait, code_sent = neighbours(
        remote(codes, codes_in.at[0], code_sem.at[0], code_sem.at[1], up),
        remote(codes, codes_in.at[1], code_sem.at[2], code_sem.at[3], down),
    )
    code_start()

    near_start, near_wait, near_sent = neighbours(
        remote(near_send.at[0:64], near_recv.at[0:64], near_sem.at[0], near_sem.at[1], up),
        remote(near_send.at[64:128], near_recv.at[64:128], near_sem.at[2], near_sem.at[3], down),
    )

    def couple(piece):
        return remote(
            coupled.at[piece], coupled_in.at[piece], couple_send.at[piece], couple_recv.at[piece], other_pool
        )


    @pl.when(is_coarse)
    def _():
        edges = jnp.zeros((NY, 128), F32)
        for chan in range(CH):
            pair = jnp.concatenate([fld[chan, 0], fld[chan, 1]], axis=1)
            packed[:, chan * 128 : chan * 128 + 128] = dot(pair, pack[...]).astype(BF16)
            row, col = iota((256, 128), 0), iota((256, 128), 1) - 4 * chan
            pick = (
                ((row == 31) & (col == 0))
                | ((row == 96) & (col == 1))
                | ((row == 128 + 31) & (col == 2))
                | ((row == 128 + 96) & (col == 3))
            )
            edges = edges + dot(pair, hot(pick).astype(BF16))
        packed[:, CH * 128 :] = edges.astype(BF16)

    code_wait()
    from_below, from_above = codes_in[0], codes_in[1]

    def block_columns(code):
        table = hot(iota((8, NY), 1) // ROWS == iota((8, NY), 0)).astype(BF16)
        return dot(code[:, 0:BLOCKS].astype(BF16), table)

    def block_rows(code):
        table = hot(iota((NY, 8), 0) // ROWS == iota((NY, 8), 1)).astype(BF16)
        return dot_nt(table, code[:, 0:BLOCKS].astype(BF16))

    own_rows = block_rows(codes[...])

    @pl.when(is_coarse)
    def _():
        for part, row in ((0, block_columns(from_above)[0:1]), (1, block_columns(from_below)[1:2])):
            slot, cell = iota((64, NY), 0), iota((64, NY), 1)
            pick = ((slot // ROWS).astype(F32) == row) & (lax.rem(slot, ROWS) == lax.rem(cell, ROWS))
            chosen = dot(hot(pick).astype(BF16), packed[...])
            near_send[part * 64 : part * 64 + 64, :] = chosen.astype(BF16)
        near_start()

    spread = dot(
        lin[...], hot((iota((2 * CH, 256), 1) // 8) == iota((2 * CH, 256), 0)).astype(BF16)
    )
    shift = dot_tn(
        jnp.broadcast_to(bias[...], (8, CH)),
        hot((iota((8, 256), 0) == 0) & (iota((8, 256), 1) == 160)).astype(BF16),
    )
    per_row = dot(
        hot((iota((80, CH), 0) // 8) == iota((80, CH), 1)).astype(BF16), (spread + shift).astype(BF16)
    )
    keep = (lax.rem(iota((80, 256), 0), 8) == lax.rem(iota((80, 256), 1), 8)) | (
        iota((80, 256), 1) == 160
    )
    lin_left[...] = jnp.where(keep, per_row, 0.0).astype(BF16)

    below_rows, above_rows = block_rows(from_below), block_rows(from_above)
    gy_all = gy[...].astype(F32)
    coarse_scale = jnp.where(is_coarse, 1.0, 0.0)
    left[:, 0:64] = gy[...]
    for part, mask in (
        (1, own_rows[:, 2:3]),
        (2, below_rows[:, 1:2]),
        (3, above_rows[:, 0:1]),
    ):
        left[:, part * 64 : part * 64 + 64] = (gy_all * (hot(mask > -0.5) * coarse_scale)).astype(BF16)
    right[...] = jnp.zeros(right.shape, BF16)
    mixed[...] = jnp.zeros(mixed.shape, BF16)

    z_wait()
    send_w[...] = dot(perm_b[...], recv_z[...]).astype(BF16)
    w_start()

    @pl.when(is_coarse)
    def _():
        near_wait()
        slot, cell = iota((NY, 128), 1), iota((NY, 128), 0)
        code = jnp.where(slot < 64, own_rows[:, 0:1], own_rows[:, 1:2])
        inner = lax.rem(slot, 64)
        pick = ((inner // ROWS).astype(F32) == code) & (lax.rem(inner, ROWS) == lax.rem(cell, ROWS))
        moved = dot(hot(pick).astype(BF16), near_recv[...])
        kept = hot(own_rows[:, 2:3] > -0.5)
        value = (moved + packed[...].astype(F32) * kept).astype(BF16)
        for piece in range(CH + 1):
            coupled[piece] = value[:, piece * 128 : piece * 128 + 128]

    def couple_start(first, last):
        @pl.when(is_coarse)
        def _():
            @pl.loop(first, last)
            def _(piece):
                couple(piece).start()

    couple_start(LATE, LATE + MIDDLE)


    load_w.wait()
    w_wait()

    spread_a = dot_tn(recv_w[...], fx[0])
    spread_b = dot_tn(recv_w[...], fx[1])
    coeffs = (spread_a[0:320] + spread_b[320:640]).astype(BF16).astype(F32)

    def mix(first, chan):
        total = jnp.zeros((32, M), F32)
        for i in range(CH):
            total = total + wts[i, first + chan].astype(F32) * coeffs[i * 32 : i * 32 + 32]
        return total

    for chan in range(CH):
        mix_send[chan] = mix((1 - ch) * CH, chan).astype(BF16)
    mix_copy = remote(mix_send, mix_recv, mix_sem.at[0], mix_sem.at[1], twin)
    mix_copy.start()
    own = [mix(ch * CH, chan) for chan in range(CH)]
    mix_copy.wait_recv()
    for chan in range(CH):
        value = (own[chan] + mix_recv[chan].astype(F32)).astype(BF16)
        mixed[0, chan * 32 : chan * 32 + 32, :] = value
        mixed[1, 320 + chan * 32 : 320 + chan * 32 + 32, :] = value
    send_v[...] = (dot_nt(gx[0], mixed[0]) + dot_nt(gx[1], mixed[1])).astype(BF16)
    v_start()
    v_wait()
    send_u[...] = dot_tn(perm_b[...], recv_v[...]).astype(BF16)
    u_start()
    couple_start(0, LATE)

    to_peer.wait_recv()
    ones_row = hot(iota((16, 256), 0) == 0).astype(BF16)

    def channel_map(first, second):
        @pl.loop(0, NY // 8)
        def _(block):
            here = pl.ds(pl.multiple_of(block * 8, 8), 8)
            planes = []
            for plane in range(PLANES):
                planes.append(
                    jnp.concatenate(
                        [first[chan, plane, here, :] for chan in range(CH)]
                        + [second[chan, plane, here, :] for chan in range(CH)],
                        axis=0,
                    )
                )
            cells = jnp.concatenate([jnp.concatenate(planes, axis=1), ones_row], axis=0)
            total = dot(lin_left[:, 0:176], cells)
            for chan in range(CH):
                base[chan, here, :] = total[chan * 8 : chan * 8 + 8]

    @pl.when(ch == 0)
    def _():
        channel_map(fld, peer)

    @pl.when(ch == 1)
    def _():
        channel_map(peer, fld)


    def interpolate(first, last):
        @pl.loop(first, last)
        def _(chan):
            couple(chan).wait_recv()
            cells = coupled_in[chan]
            row, col = iota((128, 256), 0) - 4 * chan, iota((128, 256), 1)
            pick = (
                ((row == 0) & (col == 0))
                | ((row == 1) & (col == 127))
                | ((row == 2) & (col == 128))
                | ((row == 3) & (col == 255))
            )
            value = dot(cells, unpack[...]) + dot(
                coupled_in[CH], jnp.where(pick, 0.25, 0.0).astype(BF16)
            )
            base[chan] = base[chan] + value.astype(BF16).astype(F32)

    @pl.when(pool == 1)
    def _():
        couple(CH).wait_recv()
        interpolate(LATE, CH)

    def expand(sources, table, parts):
        lefts = []
        for rows in sources:
            ordered = dot_tn(perm_a[...], rows).astype(BF16)
            for group in range(5):
                lefts.append(
                    jnp.concatenate(
                        [ordered[half * 64 : half * 64 + 64, group * 128 : group * 128 + 128] for half in range(2)],
                        axis=1,
                    )
                )
        value = dot(jnp.concatenate(lefts, axis=0), table).astype(BF16)
        for index, part in enumerate(parts):
            for group in range(5):
                first = (index * 5 + group) * 64
                for lane in range(4):
                    plane, chan = (group * 4 + lane) // CH, (group * 4 + lane) % CH
                    right[chan, part * 64 : part * 64 + 64, plane * 128 : plane * 128 + 128] = value[
                        first : first + 64, lane * 128 : lane * 128 + 128
                    ]

    def near_first(step):
        apart = ((step + 1) // 2) * (1 - 2 * lax.rem(step, 2))
        return lax.rem(zed + apart + RZ, RZ)

    def chunk(ref, index):
        return ref.at[pl.ds(pl.multiple_of(index * 8, 8), 8), :]

    def modes_out(origin):
        return remote(
            chunk(recv_u, origin), chunk(modes_in.at[0], origin), out_send.at[origin], out_recv.at[origin], other_pool
        )

    def modes_near(origin):
        source_ref = chunk(modes_in.at[0], origin)
        return neighbours(
            remote(source_ref, chunk(modes_in.at[1], origin), up_send.at[origin], up_recv.at[origin], up),
            remote(source_ref, chunk(modes_in.at[2], origin), down_send.at[origin], down_recv.at[origin], down),
        )

    @pl.loop(0, RZ)
    def _(step):
        origin = near_first(step)

        @pl.when((origin != zed) & (pool == 1))
        def _():
            u_from(origin).wait_recv()

        @pl.when(pool == 1)
        def _():
            modes_out(origin).start()

        @pl.when(is_coarse)
        def _():
            modes_out(origin).wait_recv()
            modes_near(origin)[0]()

    @pl.when(is_coarse)
    def _():
        @pl.loop(1, RZ)
        def _(step):
            u_from(lax.rem(zed + step, RZ)).wait_recv()

    expand((recv_u[...],), bdi[...], (0,))

    @pl.when(is_coarse)
    def _():
        expand((modes_in[0],), bdc[...], (1,))

        @pl.loop(0, RZ)
        def _(step):
            modes_near(near_first(step))[1]()

        expand((modes_in[1], modes_in[2]), bdc[...], (2, 3))

    @pl.when(pool == 1)
    def _():
        interpolate(0, LATE)

    def store(chan):
        return pltpu.make_async_copy(result.at[chan], out.at[0, chan], out_sem.at[chan])

    @pl.loop(0, CH, unroll=5)
    def _(chan):
        total = dot(left[...], right[chan]) + base[chan]
        value = (total * (1.0 + lax.erf(total * np.float32(np.sqrt(0.5)))) * 0.5).astype(BF16)
        for plane in range(PLANES):
            result[chan, plane] = value[:, plane * 128 : plane * 128 + 128]
        store(chan).start()

    z_sent()
    w_sent()
    v_sent()
    u_sent()
    code_sent()
    to_peer.wait_send()
    mix_copy.wait_send()

    @pl.when(is_coarse)
    def _():
        near_sent()

        @pl.loop(0, CH + 1)
        def _(piece):
            couple(piece).wait_send()

        @pl.loop(0, RZ)
        def _(step):
            modes_near(near_first(step))[2]()

    @pl.when(pool == 1)
    def _():
        @pl.loop(0, RZ)
        def _(step):
            modes_out(near_first(step)).wait_send()

    @pl.loop(0, CH)
    def _(chan):
        store(chan).wait()


def body(fields, mode_weights, lin_weights, bias, source):
    weights = jnp.swapaxes(mode_weights[0], 2, 3)
    lin = jnp.swapaxes(lin_weights[0], 0, 1)
    tables = make_tables()
    anywhere = pl.BlockSpec(memory_space=pl.ANY)
    dma = pltpu.SemaphoreType.DMA
    scratch = [pltpu.VMEM(lin.shape, BF16), pltpu.VMEM(bias.shape, BF16), pltpu.VMEM(source.shape, jnp.int32)]
    scratch += [pltpu.VMEM(table.shape, BF16) for table in tables] + [
        pltpu.VMEM((CH, PLANES, NY, NZ), BF16),
        pltpu.VMEM((CH, PLANES, NY, NZ), BF16),
        pltpu.VMEM((CH, 2 * CH, 32, M), BF16),
        pltpu.VMEM((320, 512), BF16),
        pltpu.VMEM((128, LANES), BF16),
        pltpu.VMEM((128, LANES), BF16),
        pltpu.VMEM((128, LANES), BF16),
        pltpu.VMEM((128, LANES), BF16),
        pltpu.VMEM((128, LANES), BF16),
        pltpu.VMEM((CH, 32, M), BF16),
        pltpu.VMEM((CH, 32, M), BF16),
        pltpu.VMEM((2, LANES, M), BF16),
        pltpu.VMEM((128, LANES), BF16),
        pltpu.VMEM((128, LANES), BF16),
        pltpu.VMEM((128, LANES), BF16),
        pltpu.VMEM((128, LANES), BF16),
        pltpu.VMEM((8, 128), F32),
        pltpu.VMEM((2, 8, 128), F32),
        pltpu.VMEM((CH, NY, 256), F32),
        pltpu.VMEM((80, 256), BF16),
        pltpu.VMEM((NY, PACKED), BF16),
        pltpu.VMEM((128, PACKED), BF16),
        pltpu.VMEM((128, PACKED), BF16),
        pltpu.VMEM((CH + 1, NY, 128), BF16),
        pltpu.VMEM((CH + 1, NY, 128), BF16),
        pltpu.VMEM((3, 128, LANES), BF16),
        pltpu.VMEM((NY, 256), BF16),
        pltpu.VMEM((CH, 256, 256), BF16),
        pltpu.VMEM((CH, PLANES, NY, NZ), BF16),
        dma, dma,
        dma((RZ,)), dma((RZ,)), dma((RW,)), dma((RW,)), dma((RW,)), dma((RW,)), dma((RZ,)), dma((RZ,)),
        dma((2,)), dma((4,)), dma((2,)), dma((4,)), dma((CH + 1,)), dma((CH + 1,)), dma((len(NAMES) + 3,)),
        dma((RZ,)), dma((RZ,)), dma((RZ,)), dma((RZ,)), dma((RZ,)), dma((RZ,)), dma((CH,)),
    ]
    return pl.pallas_call(
        kernel,
        out_shape=jax.ShapeDtypeStruct(fields.shape, BF16),
        in_specs=[anywhere] * (5 + len(NAMES)),
        out_specs=anywhere,
        scratch_shapes=scratch,
        compiler_params=pltpu.CompilerParams(
            collective_id=0, has_side_effects=True, vmem_limit_bytes=60 * 2**20
        ),
    )(fields, weights, lin, bias, source, *tables)


def solution(mesh):
    return jax.shard_map(
        body,
        mesh=mesh,
        in_specs=(
            P("pool", "ch", "slab", None, None),
            P("pool", "ch", None, None, "slab"),
            P("pool", None, "ch"),
            P("pool", "ch"),
            P("slab", None),
        ),
        out_specs=P("pool", "ch", "slab", None, None),
        check_vma=False,
    )
```
